256 devices in a mesh: seq: 32 (over y, z_hi, core), head: 8 (over x, z_lo).
Axes of the slice: x: 4, y: 4, z: 8 (z_hi: 4, z_lo: 2; z = z_hi * 2 + z_lo), core: 2. Of those that a mesh axis runs over, the one named last changes fastest.
Arguments:
- tokens: bfloat16 [12288, 3072], P('seq'), may hold values from -70 to 70
- survive: int32 [12288], P('seq'), may hold values from 0 to 1, as said below
- norm_gain: float32 [3072], replicated, may hold values from 0.3 to 3
- w_qkv: bfloat16 [3072, 3, 3072], P(None, None, 'head'), may hold values from -0.109375 to 0.109375
- qk_gain: float32 [2, 24, 128], P(None, 'head'), may hold values from 0.5 to 2
- w_out: bfloat16 [3072, 3072], P('head'), may hold values from -0.109375 to 0.109375
Outputs:
- update: bfloat16 [12288, 3072], P('seq', 'head')
The draws below stay inside these ranges and needn't reach their ends.
Inputs may be any that keep to these rules, and one draw needn't show every extreme that they name: `survive`: exactly 6144 tokens run in all. The 384 positions of one sequence shard hold anywhere from none to all 384 running tokens; in every draw some shard holds all 384 and some shard none.
All inputs are finite; a program needn't handle non-finite values.
Results may differ from the reference program's by a relative error of at most 0.015.
Values may be sent and summed in bfloat16 or wider, within the bound.
A program may use at most 128 MiB of HBM per device.

```python
import math
import jax
import jax.numpy as jnp
from jax import lax

MODEL_WIDTH = 3072
HEAD_COUNT = 24
HEAD_WIDTH = 128
KEEP_DEV = 192
ALL_HEAD_WIDTH = 3072
POS_DEV = 384
WINDOW_LENGTH = 12288
RUNNING_TOKENS = 6144


def draw_tokens(key, part):
    key_base, key_column, key_row = jax.random.split(jax.random.fold_in(key, 23), 3)
    gaussian = jax.random.truncated_normal(key_base, -4.0, 4.0, (WINDOW_LENGTH, MODEL_WIDTH), jnp.float32)
    column_scale = jnp.exp(jax.random.uniform(key_column, (1, MODEL_WIDTH), jnp.float32, math.log(0.3), math.log(3.0)))
    row_scale = jnp.exp(jax.random.uniform(key_row, (WINDOW_LENGTH, 1), jnp.float32, math.log(0.5), math.log(5.0)))
    values = gaussian * column_scale * row_scale
    return values.astype(jnp.bfloat16)


def draw_survive(key, part):
    key_swing, key_order, key_ranks = jax.random.split(jax.random.fold_in(key, 11), 3)
    shard_total = WINDOW_LENGTH // POS_DEV
    pair_count = shard_total // 2
    pair_swing = jax.random.randint(key_swing, (pair_count,), 0, KEEP_DEV + 1)
    pair_swing = pair_swing.at[0].set(KEEP_DEV)
    shard_counts = jnp.concatenate([KEEP_DEV + pair_swing, KEEP_DEV - pair_swing])
    shard_order = jax.random.permutation(key_order, shard_total)
    shard_counts = shard_counts[shard_order]
    position_ranks = jax.vmap(lambda sub_key: jax.random.permutation(sub_key, POS_DEV))(jax.random.split(key_ranks, shard_total))
    alive = (position_ranks < shard_counts[:, None]).astype(jnp.int32)
    return alive.reshape(WINDOW_LENGTH)


def levels(key, shape, cuts, least, top_value):
    level, own = 1.0, jax.random.fold_in(key, 6)
    for position, parts in cuts:
        draws = jnp.exp(jax.random.uniform(jax.random.fold_in(own, position), (parts,), jnp.float32, least / len(cuts), top_value / len(cuts)))
        level = level * jnp.repeat(draws, shape[position] // parts).reshape([-1 if axis == position else 1 for axis in range(len(shape))])
    return level


def normal_values(key, dims, width, bound, shards=(), kind=jnp.bfloat16):
    loudness = levels(key, dims, shards, -0.22, 0.18) if shards else 1.0
    entries = jax.random.normal(key, dims, jnp.float32) * width * loudness
    return jnp.minimum(jnp.maximum(entries, -bound), bound).astype(kind)


def setup_inputs(seed: int = 0) -> dict:
    arg_keys = jax.random.split(jax.random.key(seed), 7)
    return {
        "tokens": draw_tokens(jax.random.fold_in(arg_keys[6], 71), 0),
        "survive": draw_survive(jax.random.fold_in(arg_keys[6], 71), 0),
        "norm_gain": jnp.clip(jnp.exp(jax.random.uniform(arg_keys[2], (MODEL_WIDTH,), jnp.float32, math.log(0.3), math.log(3.0))), 0.3, 3.0),
        "w_qkv": normal_values(arg_keys[3], (MODEL_WIDTH, 3, ALL_HEAD_WIDTH), MODEL_WIDTH ** -0.5, 0.109375, ((2, 8),)),
        "qk_gain": jnp.clip(jnp.exp(math.log(2.0) - 1.3862944 * jax.random.uniform(arg_keys[4], (2, HEAD_COUNT, HEAD_WIDTH), jnp.float32) ** levels(arg_keys[4], (2, HEAD_COUNT, HEAD_WIDTH), ((1, 8),), -0.2, 0.2)), 0.5, 2.0),
        "w_out": normal_values(arg_keys[5], (ALL_HEAD_WIDTH, MODEL_WIDTH), ALL_HEAD_WIDTH ** -0.5, 0.109375, ((0, 8),)),
    }


epsilon = 1e-06

def layer_norm(values, gain):
    center = values - lax.optimization_barrier(jnp.mean(values, axis=-1, keepdims=True))
    spread = lax.optimization_barrier(jnp.mean(center * center, axis=-1, keepdims=True))
    return center * lax.rsqrt(spread + epsilon) * gain

def reference(tokens, survive, norm_gain, w_qkv, qk_gain, w_out):
    running_token_index = jnp.argsort(1 - survive, stable=True)[:RUNNING_TOKENS].astype(jnp.int32)
    source_tokens = tokens[running_token_index].astype(jnp.float32)
    normed = layer_norm(source_tokens, norm_gain).astype(jnp.bfloat16)
    projected_output = jnp.dot(normed, w_qkv.reshape(MODEL_WIDTH, 3 * ALL_HEAD_WIDTH), preferred_element_type=jnp.float32)
    query_rows = projected_output[:, :ALL_HEAD_WIDTH].reshape(RUNNING_TOKENS, HEAD_COUNT, HEAD_WIDTH)
    running_key_rows = projected_output[:, ALL_HEAD_WIDTH:2 * ALL_HEAD_WIDTH].reshape(RUNNING_TOKENS, HEAD_COUNT, HEAD_WIDTH)
    running_value_rows = projected_output[:, 2 * ALL_HEAD_WIDTH:].reshape(RUNNING_TOKENS, HEAD_COUNT, HEAD_WIDTH).astype(jnp.bfloat16)
    query_rows = layer_norm(query_rows, qk_gain[0]).astype(jnp.bfloat16)
    running_key_rows = layer_norm(running_key_rows, qk_gain[1]).astype(jnp.bfloat16)
    score_scale = 1.0 / math.sqrt(HEAD_WIDTH)

    def one_head(stacked):
        head_queries, head_keys, head_values = stacked
        scores = jnp.dot(head_queries, head_keys.T, preferred_element_type=jnp.float32) * score_scale
        weights = jnp.exp(scores)
        denominator = lax.optimization_barrier(jnp.sum(weights, axis=-1))
        numerator = jnp.dot(weights.astype(jnp.bfloat16), head_values, preferred_element_type=jnp.float32)
        return (numerator / denominator[:, None]).astype(jnp.bfloat16)
    split_per_head = lax.map(one_head, (jnp.transpose(query_rows, (1, 0, 2)), jnp.transpose(running_key_rows, (1, 0, 2)), jnp.transpose(running_value_rows, (1, 0, 2))))
    attended_output = jnp.transpose(split_per_head, (1, 0, 2)).reshape(RUNNING_TOKENS, ALL_HEAD_WIDTH)
    attention_branch = jnp.dot(attended_output, w_out, preferred_element_type=jnp.float32)
    return jnp.zeros((WINDOW_LENGTH, MODEL_WIDTH), jnp.bfloat16).at[running_token_index].set(attention_branch.astype(jnp.bfloat16))
```

```python
import math

import jax
import jax.numpy as jnp
from jax import lax
from jax.experimental import pallas as pl
from jax.experimental.pallas import tpu as pltpu
from jax.sharding import PartitionSpec as P

epsilon = 1e-06
MESH = pl.DeviceIdType.MESH
f32, bf16 = jnp.float32, jnp.bfloat16

POS = 384
WIDTH = 3072
HEADS = 3
D = 128
CH = 3
RC = POS // CH
HALF = RC // 2


def column_of(row):
    return jnp.transpose(jnp.broadcast_to(row[0:1, :], (128, 128)))


def head_norm(x, gain):
    center = x - jnp.mean(x, axis=-1, keepdims=True)
    spread = jnp.mean(center * center, axis=-1, keepdims=True)
    return center * lax.rsqrt(spread + epsilon) * gain


def kernel(
    tok_hbm, sv_ref, ng_ref, w_hbm, qg_ref, wo_hbm, out_ref,
    tok, normed, w, wo, q, kv, lrow, lv, own, dn,
    zs, zra, zrb, zfm, zfp, zt, ds, dra, dfm, dfp, dt,
    att, xs, xown, xra, xrb, xfm, xfp, xt, zls, zlr,
    lsem, ssem, rsem,
):
    s = lax.axis_index("seq")
    hd = lax.axis_index("head")
    y, zh, co = s // 8, (s // 2) % 4, s % 2
    x, zl = hd // 2, hd % 2

    def seq_at(dy, dz, flip):
        c = (1 - co) if flip else co
        return {"seq": (((y + dy) % 4) * 4 + (zh + dz) % 4) * 2 + c}

    y_next, y_prev, sib = seq_at(1, 0, False), seq_at(3, 0, False), seq_at(0, 0, True)
    z_next, z_prev = seq_at(0, 1, False), seq_at(0, 3, False)
    x_next, x_prev = {"head": ((x + 1) % 4) * 2 + zl}, {"head": ((x + 3) % 4) * 2 + zl}
    z_pair = {"head": x * 2 + (1 - zl)}
    line = [
        (sib, 1), (y_next, 2), (seq_at(1, 0, True), 3), (y_prev, 4),
        (seq_at(3, 0, True), 5), (seq_at(2, 0, False), 6), (seq_at(2, 0, True), 7),
    ]

    loads = [pltpu.make_async_copy(tok_hbm, tok, lsem.at[0])]
    for j in range(3):
        loads.append(pltpu.make_async_copy(w_hbm.at[j], w.at[j], lsem.at[1 + j]))
    for r in range(4):
        for side in range(2):
            block = ((x + r) % 4) * 2 + (zl if side == 0 else 1 - zl)
            loads.append(
                pltpu.make_async_copy(
                    wo_hbm.at[:, pl.ds(pl.multiple_of(block * POS, 128), POS)],
                    wo.at[r, :, pl.ds(side * POS, POS)],
                    lsem.at[4 + 2 * r + side],
                )
            )
    for load in loads:
        load.start()

    barrier = pltpu.get_barrier_semaphore()
    peers = [p for p, _ in line] + [z_next, z_prev, x_next, x_prev, z_pair]
    for peer in peers:
        pl.semaphore_signal(barrier, inc=1, device_id=peer, device_id_type=MESH)

    count = [0]
    sent = []

    def message(src, dst, peer):
        i = count[0]
        count[0] += 1
        copy = pltpu.make_async_remote_copy(
            src_ref=src, dst_ref=dst, send_sem=ssem.at[i], recv_sem=rsem.at[i],
            device_id=peer, device_id_type=MESH,
        )
        sent.append(copy)
        return copy

    live = jnp.broadcast_to((sv_ref[...] == 1).astype(f32), (8, POS))
    lrow[0] = live
    for t in range(3):
        lv[0, t * 128 : (t + 1) * 128, :] = column_of(live[:, t * 128 : (t + 1) * 128]).astype(bf16)

    loads[0].wait()

    def norm_rows(i, carry):
        rows = pl.ds(pl.multiple_of(i * 16, 16), 16)
        v = tok[rows, :].astype(f32)
        center = v - jnp.mean(v, axis=-1, keepdims=True)
        spread = jnp.mean(center * center, axis=-1, keepdims=True)
        normed[rows, :] = (center * lax.rsqrt(spread + epsilon) * ng_ref[...]).astype(bf16)
        return carry

    lax.fori_loop(0, POS // 16, norm_rows, 0)

    loads[1].wait()
    projected = jnp.dot(normed[...], w[0], preferred_element_type=f32)
    score_scale = math.log2(math.e) / math.sqrt(D)
    for h in range(HEADS):
        gain = qg_ref[h, 0:1, :] * score_scale
        q[h, 0] = head_norm(projected[:, h * D : (h + 1) * D], gain).astype(bf16)

    pl.semaphore_wait(barrier, len(peers))

    live_msg = [message(lrow.at[0], lrow.at[slot], peer) for peer, slot in line]
    for m in live_msg:
        m.start()

    q_next = [message(q.at[h, 0], q.at[h, 1], z_next) for h in range(HEADS)]
    q_prev = [message(q.at[h, 0], q.at[h, 2], z_prev) for h in range(HEADS)]
    lo, hi = pl.ds(0, POS // 2), pl.ds(POS // 2, POS // 2)
    q_fwd_next = [message(q.at[h, 1, lo], q.at[h, 3, lo], z_next) for h in range(HEADS)]
    q_fwd_prev = [message(q.at[h, 2, hi], q.at[h, 3, hi], z_prev) for h in range(HEADS)]
    kv_next = [message(kv.at[h, 0], kv.at[h, 2], y_next) for h in range(HEADS)]
    kv_prev = [message(kv.at[h, 0], kv.at[h, 4], y_prev) for h in range(HEADS)]
    kv_fwd_next = [message(kv.at[h, 2, lo], kv.at[h, 6, lo], y_next) for h in range(HEADS)]
    kv_fwd_prev = [message(kv.at[h, 4, hi], kv.at[h, 6, hi], y_prev) for h in range(HEADS)]
    kv_sib = [[message(kv.at[h, 2 * r], kv.at[h, 2 * r + 1], sib) for r in range(4)] for h in range(HEADS)]

    def send_q(h):
        q_next[h].start()
        q_prev[h].start()

    def send_kv(h):
        kv_next[h].start()
        kv_prev[h].start()
        kv_sib[h][0].start()

    def forward_q(h):
        q_next[h].wait_recv()
        q_fwd_next[h].start()
        q_prev[h].wait_recv()
        q_fwd_prev[h].start()

    def forward_kv(h):
        kv_next[h].wait_recv()
        kv_fwd_next[h].start()
        kv_sib[h][1].start()
        kv_prev[h].wait_recv()
        kv_fwd_prev[h].start()
        kv_sib[h][2].start()

    def share_far(h):
        kv_fwd_next[h].wait_recv()
        kv_fwd_prev[h].wait_recv()
        kv_sib[h][3].start()

    def all_in(h):
        q_fwd_next[h].wait_recv()
        q_fwd_prev[h].wait_recv()
        for m in kv_sib[h]:
            m.wait_recv()

    def project_kv(h):
        cols = pl.ds(h * D, D)
        weights = jnp.concatenate([w[1, :, cols], w[2, :, cols]], axis=1)
        projected = jnp.dot(normed[...], weights, preferred_element_type=f32)
        kv[h, 0, :, 0:D] = head_norm(projected[:, :D], qg_ref[h, 1:2, :]).astype(bf16)
        kv[h, 0, :, D:] = (projected[:, D:] * lv[0].astype(f32)).astype(bf16)

    send_q(0)
    send_q(1)
    loads[2].wait()
    loads[3].wait()
    project_kv(0)
    send_kv(0)
    project_kv(1)
    send_kv(1)
    project_kv(2)

    for m, (_, slot) in zip(live_msg, line):
        m.wait_recv()
        for t in range(3):
            lv[slot, t * 128 : (t + 1) * 128, :] = column_of(lrow[slot, :, t * 128 : (t + 1) * 128]).astype(bf16)

    def unit(h, c):
        rows = pl.ds(c * RC, RC)
        queries = jnp.concatenate([q[h, slot, rows, :] for slot in range(4)], axis=0)
        keys = kv[h, :, :, 0:D].reshape(8 * POS, D)
        scores = lax.dot_general(queries, keys, (((1,), (1,)), ((), ())), preferred_element_type=f32)
        weights = jnp.exp2(scores).astype(bf16)
        values = jnp.concatenate([kv[h, :, :, D:].reshape(8 * POS, D), lv[...].reshape(8 * POS, D)], axis=1)
        acc = jnp.dot(weights, values, preferred_element_type=f32)
        own[h, c] = acc[0:RC, 0:D]
        for slot in range(1, 4):
            zs[h, c, slot - 1] = acc[slot * RC : (slot + 1) * RC, 0:D].astype(bf16)
        for slot in range(4):
            dn[h, c, slot] = acc[slot * RC : (slot + 1) * RC, D:]

    A, B = pl.ds(0, HALF), pl.ds(HALF, HALF)
    zmsg = {}
    for h in range(HEADS):
        for c in range(CH):
            zmsg[h, c] = [
                message(zs.at[h, c, 2, A], zra.at[h, c], z_next),
                message(zs.at[h, c, 2, B], zrb.at[h, c], z_prev),
                message(zs.at[h, c, 1, B], zfm.at[h, c, B], z_next),
                message(zs.at[h, c, 0, A], zfp.at[h, c, A], z_prev),
                message(zt.at[h, c, 0], zfm.at[h, c, A], z_next),
                message(zt.at[h, c, 1], zfp.at[h, c, B], z_prev),
            ]
    dmsg = [
        [
            message(ds.at[c, 2], dra.at[c], z_next),
            message(ds.at[c, 0], dfp.at[c], z_prev),
            message(dt.at[c], dfm.at[c], z_next),
        ]
        for c in range(CH)
    ]

    def z_first(h, c):
        for m in zmsg[h, c][:4]:
            m.start()
        if h == HEADS - 1:
            lane = lax.broadcasted_iota(jnp.int32, (RC, D), 1)
            for slot in range(1, 4):
                mixed = jnp.where(lane == 0, dn[0, c, slot], jnp.where(lane == 1, dn[1, c, slot], dn[2, c, slot]))
                ds[c, slot - 1] = jnp.transpose(mixed)[0:8, :]
            dmsg[c][0].start()
            dmsg[c][1].start()

    def z_relay(h, c):
        m = zmsg[h, c]
        m[0].wait_recv()
        zt[h, c, 0] = (zra[h, c].astype(f32) + zs[h, c, 1, 0:HALF].astype(f32)).astype(bf16)
        m[4].start()
        m[1].wait_recv()
        zt[h, c, 1] = (zrb[h, c].astype(f32) + zs[h, c, 0, HALF:].astype(f32)).astype(bf16)
        m[5].start()
        if h == HEADS - 1:
            dmsg[c][0].wait_recv()
            dt[c] = dra[c] + ds[c, 1]
            dmsg[c][2].start()

    xmsg = [
        [
            message(xs.at[c, 1, A], xra.at[c], x_next),
            message(xs.at[c, 1, B], xrb.at[c], x_prev),
            message(xs.at[c, 0, B], xfm.at[c, B], x_next),
            message(xs.at[c, 2, A], xfp.at[c, A], x_prev),
            message(xt.at[c, 0], xfm.at[c, A], x_next),
            message(xt.at[c, 1], xfp.at[c, B], x_prev),
        ]
        for c in range(CH)
    ]
    zlmsg = [message(zls.at[c], zlr.at[c], z_pair) for c in range(CH)]

    def attended(c):
        dmsg[c][1].wait_recv()
        dmsg[c][2].wait_recv()
        for h in range(HEADS):
            for m in zmsg[h, c][2:]:
                m.wait_recv()
            others = dfm[c, h : h + 1, :] + dfp[c, h : h + 1, :]
            den = dn[h, c, 0] + column_of(others)
            num = own[h, c] + zfm[h, c].astype(f32) + zfp[h, c].astype(f32)
            att[c, :, h * D : (h + 1) * D] = (num / den).astype(bf16)

    def x_first(c):
        a = att[c]
        for r in (2, 1, 3, 0):
            part = jnp.dot(a, wo[r], preferred_element_type=f32)
            if r == 0:
                xown[c] = part
            else:
                xs[c, r - 1] = part.astype(bf16)
            if r == 2:
                xmsg[c][0].start()
                xmsg[c][1].start()
            elif r == 1:
                xmsg[c][2].start()
            elif r == 3:
                xmsg[c][3].start()

    def x_relay(c):
        m = xmsg[c]
        m[0].wait_recv()
        xt[c, 0] = (xra[c].astype(f32) + xs[c, 0, 0:HALF].astype(f32)).astype(bf16)
        m[4].start()
        m[1].wait_recv()
        xt[c, 1] = (xrb[c].astype(f32) + xs[c, 2, HALF:].astype(f32)).astype(bf16)
        m[5].start()

    def x_final(c):
        for m in xmsg[c][2:]:
            m.wait_recv()
        total = xown[c] + xfm[c].astype(f32) + xfp[c].astype(f32)
        xown[c] = total
        zls[c] = total[:, POS:].astype(bf16)
        zlmsg[c].start()

    def finish(c):
        zlmsg[c].wait_recv()
        share = xown[c, :, 0:POS] + zlr[c].astype(f32)
        mask = lv[0, c * RC : (c + 1) * RC, :].astype(f32)
        mask = jnp.concatenate([mask] * (POS // D), axis=1)
        out_ref[c * RC : (c + 1) * RC, :] = jnp.where(mask > 0.5, share, 0.0).astype(bf16)

    forward_q(0)
    forward_kv(0)
    send_q(2)
    send_kv(2)
    forward_q(1)
    forward_kv(1)
    share_far(0)
    all_in(0)
    unit(0, 0)
    z_first(0, 0)
    forward_q(2)
    forward_kv(2)
    unit(0, 1)
    z_first(0, 1)
    z_relay(0, 0)
    share_far(1)
    unit(0, 2)
    z_first(0, 2)
    z_relay(0, 1)
    all_in(1)
    unit(1, 0)
    z_first(1, 0)
    z_relay(0, 2)
    share_far(2)
    unit(1, 1)
    z_first(1, 1)
    z_relay(1, 0)
    unit(1, 2)
    z_first(1, 2)
    z_relay(1, 1)
    all_in(2)
    unit(2, 0)
    z_first(2, 0)
    z_relay(1, 2)
    unit(2, 1)
    z_first(2, 1)
    z_relay(2, 0)
    for load in loads[4:]:
        load.wait()
    unit(2, 2)
    z_first(2, 2)
    z_relay(2, 1)
    attended(0)
    x_first(0)
    z_relay(2, 2)
    attended(1)
    x_first(1)
    x_relay(0)
    attended(2)
    x_first(2)
    x_relay(1)
    x_final(0)
    x_relay(2)
    x_final(1)
    finish(0)
    x_final(2)
    finish(1)
    finish(2)
    for copy in sent:
        copy.wait_send()


MESSAGES = 7 + 12 + 24 + 54 + 9 + 18 + 3


def per_device(tokens, survive, norm_gain, w_qkv, qk_gain, w_out):
    vmem = lambda *shape: pltpu.VMEM(shape, bf16)
    vmem32 = lambda *shape: pltpu.VMEM(shape, f32)
    units = (HEADS, CH)
    scratch = [
        vmem(POS, WIDTH), vmem(POS, WIDTH), vmem(3, WIDTH, POS), vmem(4, POS, 2 * POS),
        vmem(HEADS, 4, POS, D), vmem(HEADS, 8, POS, 2 * D), vmem32(8, 8, POS), vmem(8, POS, D),
        vmem32(*units, RC, D), vmem32(*units, 4, RC, D),
        vmem(*units, 3, RC, D), vmem(*units, HALF, D), vmem(*units, HALF, D),
        vmem(*units, RC, D), vmem(*units, RC, D), vmem(*units, 2, HALF, D),
        vmem32(CH, 3, 8, RC), vmem32(CH, 8, RC), vmem32(CH, 8, RC), vmem32(CH, 8, RC), vmem32(CH, 8, RC),
        vmem(CH, RC, POS), vmem(CH, 3, RC, 2 * POS), vmem32(CH, RC, 2 * POS),
        vmem(CH, HALF, 2 * POS), vmem(CH, HALF, 2 * POS), vmem(CH, RC, 2 * POS), vmem(CH, RC, 2 * POS),
        vmem(CH, 2, HALF, 2 * POS), vmem(CH, RC, POS), vmem(CH, RC, POS),
        pltpu.SemaphoreType.DMA((12,)),
        pltpu.SemaphoreType.DMA((MESSAGES,)),
        pltpu.SemaphoreType.DMA((MESSAGES,)),
    ]
    in_hbm = pl.BlockSpec(memory_space=pl.ANY)
    in_vmem = pl.BlockSpec(memory_space=pltpu.VMEM)
    return pl.pallas_call(
        kernel,
        out_shape=jax.ShapeDtypeStruct((POS, POS), bf16),
        in_specs=[in_hbm, in_vmem, in_vmem, in_hbm, in_vmem, in_hbm],
        out_specs=in_vmem,
        scratch_shapes=scratch,
        compiler_params=pltpu.CompilerParams(
            collective_id=0, has_side_effects=True, vmem_limit_bytes=60 * 2**20
        ),
        name="branch",
    )(
        tokens,
        survive.reshape(1, POS),
        norm_gain.reshape(1, WIDTH),
        jnp.transpose(w_qkv, (1, 0, 2)),
        jnp.transpose(qk_gain, (1, 0, 2)),
        w_out,
    )


def solution(mesh):
    placed = (
        P("seq", None),
        P("seq"),
        P(),
        P(None, None, "head"),
        P(None, "head", None),
        P("head", None),
    )
    return jax.shard_map(
        per_device, mesh=mesh, in_specs=placed, out_specs=P("seq", "head"), check_vma=False
    )
```

```python
import math

import jax
import jax.numpy as jnp
from jax import lax
from jax.experimental import pallas as pl
from jax.experimental.pallas import tpu as pltpu
from jax.sharding import PartitionSpec as P

epsilon = 1e-06
MESH = pl.DeviceIdType.MESH
f32, bf16 = jnp.float32, jnp.bfloat16

POS = 384
WIDTH = 3072
HEADS = 3
D = 128
CH = 3
RC = POS // CH
HALF = RC // 2


def column_of(row):
    return jnp.transpose(jnp.broadcast_to(row, (128, 128)))


def head_norm(x, gain):
    center = x - jnp.mean(x, axis=-1, keepdims=True)
    spread = jnp.mean(center * center, axis=-1, keepdims=True)
    return center * lax.rsqrt(spread + epsilon) * gain


def kernel(
    tok_hbm, sv_ref, ng_ref, w_hbm, qg_ref, wo_hbm, out_ref,
    tok, normed, w, wo, q, kv, lrow, lv, own, dn,
    zs, zra, zrb, zfm, zfp, zt, ds, dra, dfm, dfp, dt,
    xa, total, zls, zlr,
    lsem, ssem, rsem,
):
    s = lax.axis_index("seq")
    hd = lax.axis_index("head")
    y, zh, co = s // 8, (s // 2) % 4, s % 2
    x, zl = hd // 2, hd % 2

    def seq_at(dy, dz, flip):
        c = (1 - co) if flip else co
        return {"seq": (((y + dy) % 4) * 4 + (zh + dz) % 4) * 2 + c}

    y_next, y_prev, sib = seq_at(1, 0, False), seq_at(3, 0, False), seq_at(0, 0, True)
    z_next, z_prev = seq_at(0, 1, False), seq_at(0, 3, False)
    x_next, x_prev, x_far = ({"head": ((x + dx) % 4) * 2 + zl} for dx in (1, 3, 2))
    z_pair = {"head": x * 2 + (1 - zl)}
    line = [
        (sib, 1), (y_next, 2), (seq_at(1, 0, True), 3), (y_prev, 4),
        (seq_at(3, 0, True), 5), (seq_at(2, 0, False), 6), (seq_at(2, 0, True), 7),
    ]

    token_loads = []
    for c in range(CH):
        rows = pl.ds(c * RC, RC)
        token_loads.append(pltpu.make_async_copy(tok_hbm.at[rows], tok.at[rows], lsem.at[c]))
    w_loads = [pltpu.make_async_copy(w_hbm.at[j], w.at[j], lsem.at[CH + j]) for j in range(3)]
    x_cols = lambda dx: pl.ds(pl.multiple_of(((x + dx) % 4) * 2 * POS, 128), 2 * POS)
    wo_load = pltpu.make_async_copy(wo_hbm.at[:, x_cols(0)], wo.at[0], lsem.at[CH + 3])
    loads = token_loads + w_loads + [wo_load]
    for load in loads:
        load.start()

    barrier = pltpu.get_barrier_semaphore()
    peers = [p for p, _ in line] + [z_next, z_prev, x_next, x_prev, x_far, z_pair]
    for peer in peers:
        pl.semaphore_signal(barrier, inc=1, device_id=peer, device_id_type=MESH)

    count = [0]
    sent = []

    def message(src, dst, peer):
        i = count[0]
        count[0] += 1
        copy = pltpu.make_async_remote_copy(
            src_ref=src, dst_ref=dst, send_sem=ssem.at[i], recv_sem=rsem.at[i],
            device_id=peer, device_id_type=MESH,
        )
        sent.append(copy)
        return copy

    lrow[0] = jnp.zeros((8, 128), f32)
    lrow[0, 0:CH, :] = (sv_ref[...] == 1).astype(f32)

    def spread_live(slot):
        for t in range(CH):
            lv[slot, t * RC : (t + 1) * RC, :] = column_of(lrow[slot, t : t + 1, :]).astype(bf16)

    spread_live(0)

    def norm_rows(i, carry):
        rows = pl.ds(pl.multiple_of(i * 16, 16), 16)
        v = tok[rows, :].astype(f32)
        center = v - jnp.mean(v, axis=-1, keepdims=True)
        spread = jnp.mean(center * center, axis=-1, keepdims=True)
        normed[rows, :] = (center * lax.rsqrt(spread + epsilon) * ng_ref[...]).astype(bf16)
        return carry

    for c in range(CH):
        token_loads[c].wait()
        lax.fori_loop(c * RC // 16, (c + 1) * RC // 16, norm_rows, 0)

    w_loads[0].wait()
    projected = jnp.dot(normed[...], w[0], preferred_element_type=f32)
    score_scale = math.log2(math.e) / math.sqrt(D)
    for h in range(HEADS):
        gain = qg_ref[h, 0:1, :] * score_scale
        q[h, 0] = head_norm(projected[:, h * D : (h + 1) * D], gain).astype(bf16)

    pl.semaphore_wait(barrier, len(peers))

    live_msg = [message(lrow.at[0], lrow.at[slot], peer) for peer, slot in line]
    core_rows = pl.ds(pl.multiple_of(co * (POS // 2), 16), POS // 2)
    wo_msg = [
        message(wo_hbm.at[core_rows, x_cols(dx)], wo.at[r, core_rows], peer)
        for dx, r, peer in ((1, 1, x_next), (3, 2, x_prev), (2, 3, x_far))
    ]
    wo_sib = [message(wo.at[r, core_rows], wo.at[r, core_rows], sib) for r in (1, 2, 3)]
    for m in live_msg + wo_msg:
        m.start()

    q_next = [message(q.at[h, 0], q.at[h, 1], z_next) for h in range(HEADS)]
    q_prev = [message(q.at[h, 0], q.at[h, 2], z_prev) for h in range(HEADS)]
    lo, hi = pl.ds(0, POS // 2), pl.ds(POS // 2, POS // 2)
    q_fwd_next = [message(q.at[h, 1, lo], q.at[h, 3, lo], z_next) for h in range(HEADS)]
    q_fwd_prev = [message(q.at[h, 2, hi], q.at[h, 3, hi], z_prev) for h in range(HEADS)]
    kv_next = [message(kv.at[h, 0], kv.at[h, 2], y_next) for h in range(HEADS)]
    kv_prev = [message(kv.at[h, 0], kv.at[h, 4], y_prev) for h in range(HEADS)]
    kv_fwd_next = [message(kv.at[h, 2, lo], kv.at[h, 6, lo], y_next) for h in range(HEADS)]
    kv_fwd_prev = [message(kv.at[h, 4, hi], kv.at[h, 6, hi], y_prev) for h in range(HEADS)]
    kv_sib = [[message(kv.at[h, 2 * r], kv.at[h, 2 * r + 1], sib) for r in range(4)] for h in range(HEADS)]

    def send_q(h):
        q_next[h].start()
        q_prev[h].start()

    def send_kv(h):
        kv_next[h].start()
        kv_prev[h].start()
        kv_sib[h][0].start()

    def forward_q(h):
        q_next[h].wait_recv()
        q_fwd_next[h].start()
        q_prev[h].wait_recv()
        q_fwd_prev[h].start()

    def forward_kv(h):
        kv_next[h].wait_recv()
        kv_fwd_next[h].start()
        kv_sib[h][1].start()
        kv_prev[h].wait_recv()
        kv_fwd_prev[h].start()
        kv_sib[h][2].start()

    def share_far(h):
        kv_fwd_next[h].wait_recv()
        kv_fwd_prev[h].wait_recv()
        kv_sib[h][3].start()

    def all_in(h):
        q_fwd_next[h].wait_recv()
        q_fwd_prev[h].wait_recv()
        for m in kv_sib[h]:
            m.wait_recv()

    def project_kv(h):
        cols = pl.ds(h * D, D)
        weights = jnp.concatenate([w[1, :, cols], w[2, :, cols]], axis=1)
        projected = jnp.dot(normed[...], weights, preferred_element_type=f32)
        kv[h, 0, :, 0:D] = head_norm(projected[:, :D], qg_ref[h, 1:2, :]).astype(bf16)
        kv[h, 0, :, D:] = (projected[:, D:] * lv[0].astype(f32)).astype(bf16)

    send_q(0)
    send_q(1)
    w_loads[1].wait()
    w_loads[2].wait()
    project_kv(0)
    send_kv(0)
    project_kv(1)
    send_kv(1)
    project_kv(2)

    for m, (_, slot) in zip(live_msg, line):
        m.wait_recv()
        spread_live(slot)

    def unit(h, c):
        rows = pl.ds(c * RC, RC)
        queries = jnp.concatenate([q[h, slot, rows, :] for slot in range(4)], axis=0)
        keys = kv[h, :, :, 0:D].reshape(8 * POS, D)
        scores = lax.dot_general(queries, keys, (((1,), (1,)), ((), ())), preferred_element_type=f32)
        weights = jnp.exp2(scores).astype(bf16)
        values = jnp.concatenate([kv[h, :, :, D:].reshape(8 * POS, D), lv[...].reshape(8 * POS, D)], axis=1)
        acc = jnp.dot(weights, values, preferred_element_type=f32)
        own[h, c] = acc[0:RC, 0:D]
        for slot in range(1, 4):
            zs[h, c, slot - 1] = acc[slot * RC : (slot + 1) * RC, 0:D].astype(bf16)
        for slot in range(4):
            dn[h, c, slot] = acc[slot * RC : (slot + 1) * RC, D:]

    A, B = pl.ds(0, HALF), pl.ds(HALF, HALF)
    zmsg = {}
    for h in range(HEADS):
        for c in range(CH):
            zmsg[h, c] = [
                message(zs.at[h, c, 2, A], zra.at[h, c], z_next),
                message(zs.at[h, c, 2, B], zrb.at[h, c], z_prev),
                message(zs.at[h, c, 1, B], zfm.at[h, c, B], z_next),
                message(zs.at[h, c, 0, A], zfp.at[h, c, A], z_prev),
                message(zt.at[h, c, 0], zfm.at[h, c, A], z_next),
                message(zt.at[h, c, 1], zfp.at[h, c, B], z_prev),
            ]
    dmsg = {}
    for h in range(HEADS):
        for c in range(CH):
            dmsg[h, c] = [
                message(ds.at[h, c, 2], dra.at[h, c], z_next),
                message(ds.at[h, c, 0], dfp.at[h, c], z_prev),
                message(dt.at[h, c], dfm.at[h, c], z_next),
            ]

    def z_first(h, c):
        for m in zmsg[h, c][:4]:
            m.start()
        lane = lax.broadcasted_iota(jnp.int32, (RC, D), 1)
        mixed = jnp.where(lane == 0, dn[h, c, 1], jnp.where(lane == 1, dn[h, c, 2], dn[h, c, 3]))
        rows = jnp.transpose(mixed)[0:8, :]
        for i in range(3):
            ds[h, c, i] = jnp.broadcast_to(rows[i : i + 1, :], (8, RC))
        dmsg[h, c][0].start()
        dmsg[h, c][1].start()

    def z_relay(h, c):
        m = zmsg[h, c]
        m[0].wait_recv()
        zt[h, c, 0] = (zra[h, c].astype(f32) + zs[h, c, 1, 0:HALF].astype(f32)).astype(bf16)
        m[4].start()
        m[1].wait_recv()
        zt[h, c, 1] = (zrb[h, c].astype(f32) + zs[h, c, 0, HALF:].astype(f32)).astype(bf16)
        m[5].start()
        d = dmsg[h, c]
        d[0].wait_recv()
        dt[h, c] = dra[h, c] + ds[h, c, 1]
        d[2].start()

    xmsg = {}
    for h in range(HEADS):
        for c in range(CH):
            xmsg[h, c] = [
                message(xa.at[0, h, c], xa.at[1, h, c], x_next),
                message(xa.at[0, h, c], xa.at[2, h, c], x_prev),
                message(xa.at[1, h, c, A], xa.at[3, h, c, A], x_next),
                message(xa.at[2, h, c, B], xa.at[3, h, c, B], x_prev),
            ]
    zlmsg = [message(zls.at[c], zlr.at[c], z_pair) for c in range(CH)]

    def attended(h, c):
        dmsg[h, c][1].wait_recv()
        dmsg[h, c][2].wait_recv()
        for m in zmsg[h, c][2:]:
            m.wait_recv()
        den = dn[h, c, 0] + column_of(dfm[h, c, 0:1, :] + dfp[h, c, 0:1, :])
        num = own[h, c] + zfm[h, c].astype(f32) + zfp[h, c].astype(f32)
        xa[0, h, c] = (num / den).astype(bf16)
        xmsg[h, c][0].start()
        xmsg[h, c][1].start()

    def x_forward(h, c):
        m = xmsg[h, c]
        m[0].wait_recv()
        m[2].start()
        m[1].wait_recv()
        m[3].start()

    def project_out(c):
        for h in range(HEADS):
            xmsg[h, c][2].wait_recv()
            xmsg[h, c][3].wait_recv()
        rows = jnp.concatenate([xa[r, h, c] for r in range(4) for h in range(HEADS)], axis=1)
        weights = wo[...].reshape(4 * POS, 2 * POS)
        total[c] = jnp.dot(rows, weights, preferred_element_type=f32)
        other = pl.ds(pl.multiple_of((1 - zl) * POS, 128), POS)
        zls[c] = total[c, :, other].astype(bf16)
        zlmsg[c].start()

    def finish(c):
        zlmsg[c].wait_recv()
        mine = pl.ds(pl.multiple_of(zl * POS, 128), POS)
        out_ref[c * RC : (c + 1) * RC, :] = (total[c, :, mine] + zlr[c].astype(f32)).astype(bf16)

    def share_weights():
        for m, share in zip(wo_msg, wo_sib):
            m.wait_recv()
            share.start()

    steps = [(h, c) for h in range(HEADS) for c in range(CH)]

    def after(u):
        z_first(*steps[u])
        if u >= 2:
            z_relay(*steps[u - 2])
        if u >= 4:
            attended(*steps[u - 4])
        if u >= 5:
            x_forward(*steps[u - 5])

    def step(u):
        unit(*steps[u])
        after(u)

    forward_q(0)
    forward_kv(0)
    send_q(2)
    send_kv(2)
    forward_q(1)
    forward_kv(1)
    share_far(0)
    all_in(0)
    step(0)
    forward_q(2)
    forward_kv(2)
    step(1)
    share_far(1)
    step(2)
    all_in(1)
    step(3)
    share_far(2)
    step(4)
    share_weights()
    step(5)
    all_in(2)
    step(6)
    step(7)
    step(8)
    z_relay(*steps[7])
    attended(*steps[5])
    z_relay(*steps[8])
    x_forward(*steps[4])
    wo_load.wait()
    for m in wo_sib:
        m.wait_recv()
    attended(*steps[6])
    x_forward(*steps[5])
    attended(*steps[7])
    x_forward(*steps[6])
    attended(*steps[8])
    project_out(0)
    x_forward(*steps[7])
    project_out(1)
    x_forward(*steps[8])
    project_out(2)
    for c in range(CH):
        finish(c)
    for copy in sent:
        copy.wait_send()


MESSAGES = 7 + 6 + 12 + 24 + 54 + 27 + 36 + 3


def per_device(tokens, survive, norm_gain, w_qkv, qk_gain, w_out):
    vmem = lambda *shape: pltpu.VMEM(shape, bf16)
    vmem32 = lambda *shape: pltpu.VMEM(shape, f32)
    units = (HEADS, CH)
    scratch = [
        vmem(POS, WIDTH), vmem(POS, WIDTH), vmem(3, WIDTH, POS), vmem(4, POS, 2 * POS),
        vmem(HEADS, 4, POS, D), vmem(HEADS, 8, POS, 2 * D), vmem32(8, 8, 128), vmem(8, POS, D),
        vmem32(*units, RC, D), vmem32(*units, 4, RC, D),
        vmem(*units, 3, RC, D), vmem(*units, HALF, D), vmem(*units, HALF, D),
        vmem(*units, RC, D), vmem(*units, RC, D), vmem(*units, 2, HALF, D),
        vmem32(*units, 3, 8, RC), vmem32(*units, 8, RC), vmem32(*units, 8, RC), vmem32(*units, 8, RC),
        vmem32(*units, 8, RC),
        vmem(4, *units, RC, D), vmem32(CH, RC, 2 * POS), vmem(CH, RC, POS), vmem(CH, RC, POS),
        pltpu.SemaphoreType.DMA((CH + 4,)),
        pltpu.SemaphoreType.DMA((MESSAGES,)),
        pltpu.SemaphoreType.DMA((MESSAGES,)),
    ]
    in_hbm = pl.BlockSpec(memory_space=pl.ANY)
    in_vmem = pl.BlockSpec(memory_space=pltpu.VMEM)
    share = pl.pallas_call(
        kernel,
        out_shape=jax.ShapeDtypeStruct((POS, POS), bf16),
        in_specs=[in_hbm, in_vmem, in_vmem, in_hbm, in_vmem, in_hbm],
        out_specs=in_vmem,
        scratch_shapes=scratch,
        compiler_params=pltpu.CompilerParams(
            collective_id=0, has_side_effects=True, vmem_limit_bytes=60 * 2**20
        ),
        name="branch",
    )(
        tokens,
        survive.reshape(CH, RC),
        norm_gain.reshape(1, WIDTH),
        jnp.transpose(w_qkv, (1, 0, 2)),
        jnp.transpose(qk_gain, (1, 0, 2)),
        w_out,
    )
    return jnp.where(survive[:, None] == 1, share, jnp.zeros_like(share))


def solution(mesh):
    placed = (
        P("seq", None),
        P("seq"),
        P(),
        P(None, None, "head"),
        P(None, "head", None),
        P("head", None),
    )
    return jax.shard_map(
        per_device, mesh=mesh, in_specs=placed, out_specs=P("seq", "head"), check_vma=False
    )
```

```python
import math

import jax
import jax.numpy as jnp
from jax import lax
from jax.experimental import pallas as pl
from jax.experimental.pallas import tpu as pltpu
from jax.sharding import PartitionSpec as P

epsilon = 1e-06
MESH = pl.DeviceIdType.MESH
f32, bf16 = jnp.float32, jnp.bfloat16

POS = 384
WIDTH = 3072
HEADS = 3
D = 128
CH = 3
RC = POS // CH
HALF = RC // 2
DIRECT = [(2, 2)]


def column_of(row):
    return jnp.transpose(jnp.broadcast_to(row, (128, 128)))


def head_norm(x, gain):
    center = x - jnp.mean(x, axis=-1, keepdims=True)
    spread = jnp.mean(center * center, axis=-1, keepdims=True)
    return center * lax.rsqrt(spread + epsilon) * gain


def kernel(
    tok_hbm, sv_ref, ng_ref, w_hbm, qg_ref, wo_hbm, out_ref,
    tok, normed, w, wo, q, kv, lrow, lv, own, dn,
    zs, zra, zrb, zfm, zfp, zff, zt, ds, dra, dfm, dfp, dff, dt,
    xa, total, zls, zlr,
    lsem, ssem, rsem,
):
    s = lax.axis_index("seq")
    hd = lax.axis_index("head")
    y, zh, co = s // 8, (s // 2) % 4, s % 2
    x, zl = hd // 2, hd % 2

    def seq_at(dy, dz, flip):
        c = (1 - co) if flip else co
        return {"seq": (((y + dy) % 4) * 4 + (zh + dz) % 4) * 2 + c}

    y_next, y_prev, sib = seq_at(1, 0, False), seq_at(3, 0, False), seq_at(0, 0, True)
    z_next, z_prev, z_far = (seq_at(0, dz, False) for dz in (1, 3, 2))
    x_next, x_prev, x_far = ({"head": ((x + dx) % 4) * 2 + zl} for dx in (1, 3, 2))
    z_pair = {"head": x * 2 + (1 - zl)}
    line = [
        (sib, 1), (y_next, 2), (seq_at(1, 0, True), 3), (y_prev, 4),
        (seq_at(3, 0, True), 5), (seq_at(2, 0, False), 6), (seq_at(2, 0, True), 7),
    ]

    token_loads = []
    for c in range(CH):
        rows = pl.ds(c * RC, RC)
        token_loads.append(pltpu.make_async_copy(tok_hbm.at[rows], tok.at[rows], lsem.at[c]))
    w_loads = [pltpu.make_async_copy(w_hbm.at[j], w.at[j], lsem.at[CH + j]) for j in range(3)]
    x_cols = lambda dx: pl.ds(pl.multiple_of(((x + dx) % 4) * 2 * POS, 128), 2 * POS)
    wo_load = pltpu.make_async_copy(wo_hbm.at[:, x_cols(0)], wo.at[0], lsem.at[CH + 3])
    for load in token_loads + w_loads[0:1]:
        load.start()

    barrier = pltpu.get_barrier_semaphore()
    peers = [p for p, _ in line] + [z_next, z_prev, z_far, x_next, x_prev, x_far, z_pair]
    for peer in peers:
        pl.semaphore_signal(barrier, inc=1, device_id=peer, device_id_type=MESH)

    count = [0]
    sent = []

    def message(src, dst, peer):
        i = count[0]
        count[0] += 1
        copy = pltpu.make_async_remote_copy(
            src_ref=src, dst_ref=dst, send_sem=ssem.at[i], recv_sem=rsem.at[i],
            device_id=peer, device_id_type=MESH,
        )
        sent.append(copy)
        return copy

    lrow[0] = jnp.zeros((8, 128), f32)
    lrow[0, 0:CH, :] = (sv_ref[...] == 1).astype(f32)

    def spread_live(slot):
        for t in range(CH):
            lv[slot, t * RC : (t + 1) * RC, :] = column_of(lrow[slot, t : t + 1, :]).astype(bf16)

    def norm_rows(i, carry):
        rows = pl.ds(pl.multiple_of(i * 32, 32), 32)
        v = tok[rows, :].astype(f32)
        center = v - jnp.mean(v, axis=-1, keepdims=True)
        spread = jnp.mean(center * center, axis=-1, keepdims=True)
        normed[rows, :] = (center * lax.rsqrt(spread + epsilon) * ng_ref[...]).astype(bf16)
        return carry

    for c in range(CH):
        token_loads[c].wait()
        if c == CH - 1:
            for load in w_loads[1:] + [wo_load]:
                load.start()
        lax.fori_loop(c * RC // 32, (c + 1) * RC // 32, norm_rows, 0)

    score_scale = math.log2(math.e) / math.sqrt(D)

    def project_q(first, last):
        projected = jnp.dot(normed[...], w[0, :, first * D : last * D], preferred_element_type=f32)
        for h in range(first, last):
            gain = qg_ref[h, 0:1, :] * score_scale
            q[h, 0] = head_norm(projected[:, (h - first) * D : (h - first + 1) * D], gain).astype(bf16)

    w_loads[0].wait()
    project_q(0, 1)

    pl.semaphore_wait(barrier, len(peers))

    live_msg = [message(lrow.at[0], lrow.at[slot], peer) for peer, slot in line]
    core_rows = pl.ds(pl.multiple_of(co * (POS // 2), 16), POS // 2)
    wo_msg = [
        message(wo_hbm.at[core_rows, x_cols(dx)], wo.at[r, core_rows], peer)
        for dx, r, peer in ((1, 1, x_next), (3, 2, x_prev), (2, 3, x_far))
    ]
    wo_sib = [message(wo.at[r, core_rows], wo.at[r, core_rows], sib) for r in (1, 2, 3)]

    q_next = [message(q.at[h, 0], q.at[h, 1], z_next) for h in range(HEADS)]
    q_prev = [message(q.at[h, 0], q.at[h, 2], z_prev) for h in range(HEADS)]
    lo, hi = pl.ds(0, POS // 2), pl.ds(POS // 2, POS // 2)
    q_fwd_next = [message(q.at[h, 1, lo], q.at[h, 3, lo], z_next) for h in range(HEADS)]
    q_fwd_prev = [message(q.at[h, 2, hi], q.at[h, 3, hi], z_prev) for h in range(HEADS)]
    kv_next = [message(kv.at[h, 0], kv.at[h, 2], y_next) for h in range(HEADS)]
    kv_prev = [message(kv.at[h, 0], kv.at[h, 4], y_prev) for h in range(HEADS)]
    kv_fwd_next = [message(kv.at[h, 2, lo], kv.at[h, 6, lo], y_next) for h in range(HEADS)]
    kv_fwd_prev = [message(kv.at[h, 4, hi], kv.at[h, 6, hi], y_prev) for h in range(HEADS)]
    kv_sib = [[message(kv.at[h, 2 * r], kv.at[h, 2 * r + 1], sib) for r in range(4)] for h in range(HEADS)]

    def send_q(h):
        q_next[h].start()
        q_prev[h].start()

    def send_kv(h):
        kv_next[h].start()
        kv_prev[h].start()
        kv_sib[h][0].start()

    def forward_q(h):
        q_next[h].wait_recv()
        q_fwd_next[h].start()
        q_prev[h].wait_recv()
        q_fwd_prev[h].start()

    def forward_kv(h):
        kv_next[h].wait_recv()
        kv_fwd_next[h].start()
        kv_sib[h][1].start()
        kv_prev[h].wait_recv()
        kv_fwd_prev[h].start()
        kv_sib[h][2].start()

    def share_far(h):
        kv_fwd_next[h].wait_recv()
        kv_fwd_prev[h].wait_recv()
        kv_sib[h][3].start()

    def all_in(h):
        q_fwd_next[h].wait_recv()
        q_fwd_prev[h].wait_recv()
        for m in kv_sib[h]:
            m.wait_recv()

    def project_kv(h):
        cols = pl.ds(h * D, D)
        weights = jnp.concatenate([w[1, :, cols], w[2, :, cols]], axis=1)
        projected = jnp.dot(normed[...], weights, preferred_element_type=f32)
        kv[h, 0, :, 0:D] = head_norm(projected[:, :D], qg_ref[h, 1:2, :]).astype(bf16)
        kv[h, 0, :, D:] = (projected[:, D:] * lv[0].astype(f32)).astype(bf16)

    send_q(0)
    for m in live_msg + wo_msg:
        m.start()
    project_q(1, 3)
    send_q(1)
    spread_live(0)
    w_loads[1].wait()
    w_loads[2].wait()
    project_kv(0)
    send_kv(0)
    project_kv(1)
    send_kv(1)
    project_kv(2)

    for m, (_, slot) in zip(live_msg, line):
        m.wait_recv()
        spread_live(slot)

    def unit(h, c):
        rows = pl.ds(c * RC, RC)
        queries = jnp.concatenate([q[h, slot, rows, :] for slot in range(4)], axis=0)
        keys = kv[h, :, :, 0:D].reshape(8 * POS, D)
        scores = lax.dot_general(queries, keys, (((1,), (1,)), ((), ())), preferred_element_type=f32)
        weights = jnp.exp2(scores).astype(bf16)
        values = jnp.concatenate([kv[h, :, :, D:].reshape(8 * POS, D), lv[...].reshape(8 * POS, D)], axis=1)
        acc = jnp.dot(weights, values, preferred_element_type=f32)
        own[h, c] = acc[0:RC, 0:D]
        for slot in range(1, 4):
            zs[h, c, slot - 1] = acc[slot * RC : (slot + 1) * RC, 0:D].astype(bf16)
        for slot in range(4):
            dn[h, c, slot] = acc[slot * RC : (slot + 1) * RC, D:]

    A, B = pl.ds(0, HALF), pl.ds(HALF, HALF)
    zmsg, dmsg = {}, {}
    for h in range(HEADS):
        for c in range(CH):
            if (h, c) in DIRECT:
                i = DIRECT.index((h, c))
                zmsg[h, c] = [
                    message(zs.at[h, c, 2], zff.at[i], z_far),
                    message(zs.at[h, c, 1], zfm.at[h, c], z_next),
                    message(zs.at[h, c, 0], zfp.at[h, c], z_prev),
                ]
                dmsg[h, c] = [
                    message(ds.at[h, c, 2], dff.at[i], z_far),
                    message(ds.at[h, c, 1], dfm.at[h, c], z_next),
                    message(ds.at[h, c, 0], dfp.at[h, c], z_prev),
                ]
                continue
            zmsg[h, c] = [
                message(zs.at[h, c, 2, A], zra.at[h, c], z_next),
                message(zs.at[h, c, 2, B], zrb.at[h, c], z_prev),
                message(zs.at[h, c, 1, B], zfm.at[h, c, B], z_next),
                message(zs.at[h, c, 0, A], zfp.at[h, c, A], z_prev),
                message(zt.at[h, c, 0], zfm.at[h, c, A], z_next),
                message(zt.at[h, c, 1], zfp.at[h, c, B], z_prev),
            ]
            dmsg[h, c] = [
                message(ds.at[h, c, 2], dra.at[h, c], z_next),
                message(ds.at[h, c, 0], dfp.at[h, c], z_prev),
                message(dt.at[h, c], dfm.at[h, c], z_next),
            ]

    def z_first(h, c):
        for m in zmsg[h, c][:4]:
            m.start()
        lane = lax.broadcasted_iota(jnp.int32, (RC, D), 1)
        mixed = jnp.where(lane == 0, dn[h, c, 1], jnp.where(lane == 1, dn[h, c, 2], dn[h, c, 3]))
        rows = jnp.transpose(mixed)[0:8, :]
        for i in range(3):
            ds[h, c, i] = jnp.broadcast_to(rows[i : i + 1, :], (8, RC))
        for d in dmsg[h, c] if (h, c) in DIRECT else dmsg[h, c][:2]:
            d.start()

    def z_relay(h, c):
        if (h, c) in DIRECT:
            return
        m = zmsg[h, c]
        m[0].wait_recv()
        zt[h, c, 0] = (zra[h, c].astype(f32) + zs[h, c, 1, 0:HALF].astype(f32)).astype(bf16)
        m[4].start()
        m[1].wait_recv()
        zt[h, c, 1] = (zrb[h, c].astype(f32) + zs[h, c, 0, HALF:].astype(f32)).astype(bf16)
        m[5].start()
        d = dmsg[h, c]
        d[0].wait_recv()
        dt[h, c] = dra[h, c] + ds[h, c, 1]
        d[2].start()

    xmsg = {}
    for h in range(HEADS):
        for c in range(CH):
            xmsg[h, c] = [
                message(xa.at[0, h, c], xa.at[r, h, c], peer)
                for r, peer in ((3, x_far), (1, x_next), (2, x_prev))
            ]
    zlmsg = [message(zls.at[c], zlr.at[c], z_pair) for c in range(CH)]

    def attended(h, c):
        direct = (h, c) in DIRECT
        for m in dmsg[h, c][0 if direct else 1 :] + zmsg[h, c][0 if direct else 2 :]:
            m.wait_recv()
        others = dfm[h, c, 0:1, :] + dfp[h, c, 0:1, :]
        num = own[h, c] + zfm[h, c].astype(f32) + zfp[h, c].astype(f32)
        if direct:
            others = others + dff[DIRECT.index((h, c)), 0:1, :]
            num = num + zff[DIRECT.index((h, c))].astype(f32)
        den = dn[h, c, 0] + column_of(others)
        xa[0, h, c] = (num / den).astype(bf16)
        for m in xmsg[h, c]:
            m.start()

    def project_out(c):
        for h in range(HEADS):
            for m in xmsg[h, c]:
                m.wait_recv()
        rows = jnp.concatenate([xa[r, h, c] for r in range(4) for h in range(HEADS)], axis=1)
        weights = wo[...].reshape(4 * POS, 2 * POS)
        total[c] = jnp.dot(rows, weights, preferred_element_type=f32)
        other = pl.ds(pl.multiple_of((1 - zl) * POS, 128), POS)
        zls[c] = total[c, :, other].astype(bf16)
        zlmsg[c].start()

    def finish(c):
        zlmsg[c].wait_recv()
        mine = pl.ds(pl.multiple_of(zl * POS, 128), POS)
        out_ref[c * RC : (c + 1) * RC, :] = (total[c, :, mine] + zlr[c].astype(f32)).astype(bf16)

    def share_weights():
        for m, share in zip(wo_msg, wo_sib):
            m.wait_recv()
            share.start()

    steps = [(h, c) for h in range(HEADS) for c in range(CH)]

    def after(u):
        z_first(*steps[u])
        if u >= 2:
            z_relay(*steps[u - 2])
        if u >= 4:
            attended(*steps[u - 4])

    def step(u):
        unit(*steps[u])
        after(u)

    forward_q(0)
    forward_kv(0)
    send_q(2)
    send_kv(2)
    forward_q(1)
    forward_kv(1)
    share_far(0)
    all_in(0)
    step(0)
    forward_q(2)
    forward_kv(2)
    step(1)
    share_far(1)
    step(2)
    all_in(1)
    step(3)
    share_far(2)
    step(4)
    share_weights()
    step(5)
    all_in(2)
    step(6)
    step(7)
    step(8)
    z_relay(*steps[7])
    attended(*steps[5])
    z_relay(*steps[8])
    wo_load.wait()
    for m in wo_sib:
        m.wait_recv()
    attended(*steps[6])
    attended(*steps[7])
    project_out(0)
    attended(*steps[8])
    project_out(1)
    project_out(2)
    for c in range(CH):
        finish(c)
    for copy in sent:
        copy.wait_send()


MESSAGES = 7 + 6 + 12 + 24 + 54 + 27 - 3 * len(DIRECT) + 27 + 3


def per_device(tokens, survive, norm_gain, w_qkv, qk_gain, w_out):
    vmem = lambda *shape: pltpu.VMEM(shape, bf16)
    vmem32 = lambda *shape: pltpu.VMEM(shape, f32)
    units = (HEADS, CH)
    scratch = [
        vmem(POS, WIDTH), vmem(POS, WIDTH), vmem(3, WIDTH, POS), vmem(4, POS, 2 * POS),
        vmem(HEADS, 4, POS, D), vmem(HEADS, 8, POS, 2 * D), vmem32(8, 8, 128), vmem(8, POS, D),
        vmem32(*units, RC, D), vmem32(*units, 4, RC, D),
        vmem(*units, 3, RC, D), vmem(*units, HALF, D), vmem(*units, HALF, D),
        vmem(*units, RC, D), vmem(*units, RC, D), vmem(len(DIRECT), RC, D), vmem(*units, 2, HALF, D),
        vmem32(*units, 3, 8, RC), vmem32(*units, 8, RC), vmem32(*units, 8, RC), vmem32(*units, 8, RC),
        vmem32(len(DIRECT), 8, RC), vmem32(*units, 8, RC),
        vmem(4, *units, RC, D), vmem32(CH, RC, 2 * POS), vmem(CH, RC, POS), vmem(CH, RC, POS),
        pltpu.SemaphoreType.DMA((CH + 4,)),
        pltpu.SemaphoreType.DMA((MESSAGES,)),
        pltpu.SemaphoreType.DMA((MESSAGES,)),
    ]
    in_hbm = pl.BlockSpec(memory_space=pl.ANY)
    in_vmem = pl.BlockSpec(memory_space=pltpu.VMEM)
    share = pl.pallas_call(
        kernel,
        out_shape=jax.ShapeDtypeStruct((POS, POS), bf16),
        in_specs=[in_hbm, in_vmem, in_vmem, in_hbm, in_vmem, in_hbm],
        out_specs=in_vmem,
        scratch_shapes=scratch,
        compiler_params=pltpu.CompilerParams(
            collective_id=0, has_side_effects=True, vmem_limit_bytes=60 * 2**20
        ),
        name="branch",
    )(
        tokens,
        survive.reshape(CH, RC),
        norm_gain.reshape(1, WIDTH),
        jnp.transpose(w_qkv, (1, 0, 2)),
        jnp.transpose(qk_gain, (1, 0, 2)),
        w_out,
    )
    return jnp.where(survive[:, None] == 1, share, jnp.zeros_like(share))


def solution(mesh):
    placed = (
        P("seq", None),
        P("seq"),
        P(),
        P(None, None, "head"),
        P(None, "head", None),
        P("head", None),
    )
    return jax.shard_map(
        per_device, mesh=mesh, in_specs=placed, out_specs=P("seq", "head"), check_vma=False
    )
```

```python
import math

import jax
import jax.numpy as jnp
from jax import lax
from jax.experimental import pallas as pl
from jax.experimental.pallas import tpu as pltpu
from jax.sharding import PartitionSpec as P

epsilon = 1e-06
MESH = pl.DeviceIdType.MESH
f32, bf16 = jnp.float32, jnp.bfloat16

POS = 384
WIDTH = 3072
HEADS = 3
D = 128
CH = 3
RC = POS // CH
HALF = RC // 2
DIRECT = [(2, 1), (2, 2)]


def column_of(row):
    return jnp.transpose(jnp.broadcast_to(row, (128, 128)))


def head_norm(x, gain):
    center = x - jnp.mean(x, axis=-1, keepdims=True)
    spread = jnp.mean(center * center, axis=-1, keepdims=True)
    return center * lax.rsqrt(spread + epsilon) * gain


def kernel(
    tok_hbm, sv_ref, ng_ref, w_hbm, qg_ref, wo_hbm, out_ref,
    tok, normed, w, wo, q, kv, lrow, lv, own, dn,
    zs, zra, zrb, zfm, zfp, zff, zt, ds, dra, dfm, dfp, dff, dt,
    xa, total, zls, zlr,
    lsem, ssem, rsem,
):
    s = lax.axis_index("seq")
    hd = lax.axis_index("head")
    y, zh, co = s // 8, (s // 2) % 4, s % 2
    x, zl = hd // 2, hd % 2

    def seq_at(dy, dz, flip):
        c = (1 - co) if flip else co
        return {"seq": (((y + dy) % 4) * 4 + (zh + dz) % 4) * 2 + c}

    y_next, y_prev, sib = seq_at(1, 0, False), seq_at(3, 0, False), seq_at(0, 0, True)
    z_next, z_prev, z_far = (seq_at(0, dz, False) for dz in (1, 3, 2))
    x_next, x_prev, x_far = ({"head": ((x + dx) % 4) * 2 + zl} for dx in (1, 3, 2))
    z_pair = {"head": x * 2 + (1 - zl)}
    line = [
        (sib, 1), (y_next, 2), (seq_at(1, 0, True), 3), (y_prev, 4),
        (seq_at(3, 0, True), 5), (seq_at(2, 0, False), 6), (seq_at(2, 0, True), 7),
    ]

    token_loads = []
    for c in range(CH):
        rows = pl.ds(c * RC, RC)
        token_loads.append(pltpu.make_async_copy(tok_hbm.at[rows], tok.at[rows], lsem.at[c]))
    w_loads = [pltpu.make_async_copy(w_hbm.at[j], w.at[j], lsem.at[CH + j]) for j in range(3)]
    x_cols = lambda dx: pl.ds(pl.multiple_of(((x + dx) % 4) * 2 * POS, 128), 2 * POS)
    wo_load = pltpu.make_async_copy(wo_hbm.at[:, x_cols(0)], wo.at[0], lsem.at[CH + 3])
    for load in token_loads + w_loads[0:1]:
        load.start()

    barrier = pltpu.get_barrier_semaphore()
    peers = [p for p, _ in line] + [z_next, z_prev, z_far, x_next, x_prev, x_far, z_pair]
    for peer in peers:
        pl.semaphore_signal(barrier, inc=1, device_id=peer, device_id_type=MESH)

    count = [0]
    sent = []

    def message(src, dst, peer):
        i = count[0]
        count[0] += 1
        copy = pltpu.make_async_remote_copy(
            src_ref=src, dst_ref=dst, send_sem=ssem.at[i], recv_sem=rsem.at[i],
            device_id=peer, device_id_type=MESH,
        )
        sent.append(copy)
        return copy

    lrow[0] = jnp.zeros((8, 128), f32)
    lrow[0, 0:CH, :] = (sv_ref[...] == 1).astype(f32)

    def spread_live(slot):
        for t in range(CH):
            lv[slot, t * RC : (t + 1) * RC, :] = column_of(lrow[slot, t : t + 1, :]).astype(bf16)

    def norm_rows(i, carry):
        rows = pl.ds(pl.multiple_of(i * 32, 32), 32)
        v = tok[rows, :].astype(f32)
        center = v - jnp.mean(v, axis=-1, keepdims=True)
        spread = jnp.mean(center * center, axis=-1, keepdims=True)
        normed[rows, :] = (center * lax.rsqrt(spread + epsilon) * ng_ref[...]).astype(bf16)
        return carry

    score_scale = math.log2(math.e) / math.sqrt(D)
    lo, hi = pl.ds(0, POS // 2), pl.ds(POS // 2, POS // 2)
    q_next, q_prev, q_fwd_next, q_fwd_prev = [], [], [], []
    for c in range(CH):
        rows = pl.ds(c * RC, RC)
        first, second = pl.ds(c * RC, HALF), pl.ds(c * RC + HALF, HALF)
        q_next.append(message(q.at[0, :, rows], q.at[1, :, rows], z_next))
        q_prev.append(message(q.at[0, :, rows], q.at[2, :, rows], z_prev))
        q_fwd_next.append(message(q.at[1, :, first], q.at[3, :, first], z_next))
        q_fwd_prev.append(message(q.at[2, :, second], q.at[3, :, second], z_prev))

    for c in range(CH):
        token_loads[c].wait()
        if c == CH - 1:
            for load in w_loads[1:] + [wo_load]:
                load.start()
        lax.fori_loop(c * RC // 32, (c + 1) * RC // 32, norm_rows, 0)
        if c == 0:
            w_loads[0].wait()
        rows = slice(c * RC, (c + 1) * RC)
        projected = jnp.dot(normed[rows, :], w[0], preferred_element_type=f32)
        for h in range(HEADS):
            gain = qg_ref[h, 0:1, :] * score_scale
            q[0, h, rows, :] = head_norm(projected[:, h * D : (h + 1) * D], gain).astype(bf16)
        if c == 0:
            pl.semaphore_wait(barrier, len(peers))
        q_next[c].start()
        q_prev[c].start()

    live_msg = [message(lrow.at[0], lrow.at[slot], peer) for peer, slot in line]
    core_rows = pl.ds(pl.multiple_of(co * (POS // 2), 16), POS // 2)
    wo_msg = [
        message(wo_hbm.at[core_rows, x_cols(dx)], wo.at[r, core_rows], peer)
        for dx, r, peer in ((1, 1, x_next), (3, 2, x_prev), (2, 3, x_far))
    ]
    wo_sib = [message(wo.at[r, core_rows], wo.at[r, core_rows], sib) for r in (1, 2, 3)]

    kv_next = [[message(kv.at[h, 0, half], kv.at[h, 2, half], y_next) for half in (lo, hi)] for h in range(HEADS)]
    kv_prev = [[message(kv.at[h, 0, half], kv.at[h, 4, half], y_prev) for half in (hi, lo)] for h in range(HEADS)]
    kv_fwd_next = [message(kv.at[h, 2, lo], kv.at[h, 6, lo], y_next) for h in range(HEADS)]
    kv_fwd_prev = [message(kv.at[h, 4, hi], kv.at[h, 6, hi], y_prev) for h in range(HEADS)]
    kv_sib = [[message(kv.at[h, 2 * r], kv.at[h, 2 * r + 1], sib) for r in range(4)] for h in range(HEADS)]

    def send_kv(h, part):
        kv_next[h][part].start()
        kv_prev[h][part].start()

    def forward_q(c):
        q_next[c].wait_recv()
        q_fwd_next[c].start()
        q_prev[c].wait_recv()
        q_fwd_prev[c].start()

    def forward_kv(h):
        kv_next[h][0].wait_recv()
        kv_fwd_next[h].start()
        kv_prev[h][0].wait_recv()
        kv_fwd_prev[h].start()

    def share_near(h):
        kv_next[h][1].wait_recv()
        kv_sib[h][1].start()
        kv_prev[h][1].wait_recv()
        kv_sib[h][2].start()

    def share_far(h):
        kv_fwd_next[h].wait_recv()
        kv_fwd_prev[h].wait_recv()
        kv_sib[h][3].start()

    def queries_in(c):
        q_fwd_next[c].wait_recv()
        q_fwd_prev[c].wait_recv()

    def all_in(h):
        for m in kv_sib[h]:
            m.wait_recv()

    def project_kv(h):
        cols = pl.ds(h * D, D)
        weights = jnp.concatenate([w[1, :, cols], w[2, :, cols]], axis=1)
        projected = jnp.dot(normed[...], weights, preferred_element_type=f32)
        kv[h, 0, :, 0:D] = head_norm(projected[:, :D], qg_ref[h, 1:2, :]).astype(bf16)
        kv[h, 0, :, D:] = (projected[:, D:] * lv[0].astype(f32)).astype(bf16)

    for m in live_msg + wo_msg:
        m.start()
    spread_live(0)
    w_loads[1].wait()
    w_loads[2].wait()
    project_kv(0)
    send_kv(0, 0)
    send_kv(0, 1)
    kv_sib[0][0].start()
    project_kv(1)
    send_kv(1, 0)
    kv_sib[1][0].start()
    forward_q(0)
    project_kv(2)
    kv_sib[2][0].start()
    for m, (_, slot) in zip(live_msg[:3], line[:3]):
        m.wait_recv()
        spread_live(slot)
    forward_kv(0)
    send_kv(1, 1)
    send_kv(2, 0)
    for m, (_, slot) in zip(live_msg[3:], line[3:]):
        m.wait_recv()
        spread_live(slot)

    def unit(h, c):
        rows = pl.ds(c * RC, RC)
        queries = jnp.concatenate([q[slot, h, rows, :] for slot in range(4)], axis=0)
        keys = kv[h, :, :, 0:D].reshape(8 * POS, D)
        scores = lax.dot_general(queries, keys, (((1,), (1,)), ((), ())), preferred_element_type=f32)
        weights = jnp.exp2(scores).astype(bf16)
        values = jnp.concatenate([kv[h, :, :, D:].reshape(8 * POS, D), lv[...].reshape(8 * POS, D)], axis=1)
        acc = jnp.dot(weights, values, preferred_element_type=f32)
        own[h, c] = acc[0:RC, 0:D]
        for slot in range(1, 4):
            zs[h, c, slot - 1] = acc[slot * RC : (slot + 1) * RC, 0:D].astype(bf16)
        for slot in range(4):
            dn[h, c, slot] = acc[slot * RC : (slot + 1) * RC, D:]

    A, B = pl.ds(0, HALF), pl.ds(HALF, HALF)
    zmsg, dmsg = {}, {}
    for h in range(HEADS):
        for c in range(CH):
            if (h, c) in DIRECT:
                i = DIRECT.index((h, c))
                zmsg[h, c] = [
                    message(zs.at[h, c, 2], zff.at[i], z_far),
                    message(zs.at[h, c, 1], zfm.at[h, c], z_next),
                    message(zs.at[h, c, 0], zfp.at[h, c], z_prev),
                ]
                dmsg[h, c] = [
                    message(ds.at[h, c, 2], dff.at[i], z_far),
                    message(ds.at[h, c, 1], dfm.at[h, c], z_next),
                    message(ds.at[h, c, 0], dfp.at[h, c], z_prev),
                ]
                continue
            zmsg[h, c] = [
                message(zs.at[h, c, 2, A], zra.at[h, c], z_next),
                message(zs.at[h, c, 2, B], zrb.at[h, c], z_prev),
                message(zs.at[h, c, 1, B], zfm.at[h, c, B], z_next),
                message(zs.at[h, c, 0, A], zfp.at[h, c, A], z_prev),
                message(zt.at[h, c, 0], zfm.at[h, c, A], z_next),
                message(zt.at[h, c, 1], zfp.at[h, c, B], z_prev),
            ]
            dmsg[h, c] = [
                message(ds.at[h, c, 2], dra.at[h, c], z_next),
                message(ds.at[h, c, 0], dfp.at[h, c], z_prev),
                message(dt.at[h, c], dfm.at[h, c], z_next),
            ]

    def z_first(h, c):
        for m in zmsg[h, c][:4]:
            m.start()
        lane = lax.broadcasted_iota(jnp.int32, (RC, D), 1)
        mixed = jnp.where(lane == 0, dn[h, c, 1], jnp.where(lane == 1, dn[h, c, 2], dn[h, c, 3]))
        rows = jnp.transpose(mixed)[0:8, :]
        for i in range(3):
            ds[h, c, i] = rows[i : i + 1, :]
        for d in dmsg[h, c] if (h, c) in DIRECT else dmsg[h, c][:2]:
            d.start()

    def z_relay(h, c):
        if (h, c) in DIRECT:
            return
        m = zmsg[h, c]
        m[0].wait_recv()
        zt[h, c, 0] = (zra[h, c].astype(f32) + zs[h, c, 1, 0:HALF].astype(f32)).astype(bf16)
        m[4].start()
        m[1].wait_recv()
        zt[h, c, 1] = (zrb[h, c].astype(f32) + zs[h, c, 0, HALF:].astype(f32)).astype(bf16)
        m[5].start()
        d = dmsg[h, c]
        d[0].wait_recv()
        dt[h, c] = dra[h, c] + ds[h, c, 1]
        d[2].start()

    xmsg = {}
    for h in range(HEADS):
        for c in range(CH):
            xmsg[h, c] = [
                message(xa.at[0, h, c], xa.at[r, h, c], peer)
                for r, peer in ((3, x_far), (1, x_next), (2, x_prev))
            ]
    zlmsg = [message(zls.at[c], zlr.at[c], z_pair) for c in range(CH)]

    def attended(h, c):
        direct = (h, c) in DIRECT
        for m in dmsg[h, c][0 if direct else 1 :] + zmsg[h, c][0 if direct else 2 :]:
            m.wait_recv()
        others = dfm[h, c] + dfp[h, c]
        num = own[h, c] + zfm[h, c].astype(f32) + zfp[h, c].astype(f32)
        if direct:
            others = others + dff[DIRECT.index((h, c))]
            num = num + zff[DIRECT.index((h, c))].astype(f32)
        den = dn[h, c, 0] + column_of(others)
        xa[0, h, c] = (num / den).astype(bf16)
        for m in xmsg[h, c]:
            m.start()

    def project_out(c):
        for h in range(HEADS):
            for m in xmsg[h, c]:
                m.wait_recv()
        rows = jnp.concatenate([xa[r, h, c] for r in range(4) for h in range(HEADS)], axis=1)
        other = pl.ds(pl.multiple_of((1 - zl) * POS, 128), POS)
        mine = pl.ds(pl.multiple_of(zl * POS, 128), POS)
        theirs = wo[:, :, other].reshape(4 * POS, POS)
        zls[c] = jnp.dot(rows, theirs, preferred_element_type=f32).astype(bf16)
        zlmsg[c].start()
        total[c] = jnp.dot(rows, wo[:, :, mine].reshape(4 * POS, POS), preferred_element_type=f32)

    def finish(c):
        zlmsg[c].wait_recv()
        out_ref[c * RC : (c + 1) * RC, :] = (total[c] + zlr[c].astype(f32)).astype(bf16)

    def share_weights():
        for m, share in zip(wo_msg, wo_sib):
            m.wait_recv()
            share.start()

    steps = [(h, c) for h in range(HEADS) for c in range(CH)]

    def after(u):
        z_first(*steps[u])
        if u >= 2:
            z_relay(*steps[u - 2])
        if u >= 4:
            attended(*steps[u - 4])

    def step(u):
        unit(*steps[u])
        after(u)

    share_near(0)
    forward_q(1)
    forward_kv(1)
    send_kv(2, 1)
    share_far(0)
    queries_in(0)
    all_in(0)
    step(0)
    forward_q(2)
    share_near(1)
    forward_kv(2)
    queries_in(1)
    step(1)
    share_far(1)
    share_near(2)
    queries_in(2)
    step(2)
    all_in(1)
    share_far(2)
    step(3)
    step(4)
    share_weights()
    step(5)
    all_in(2)
    step(6)
    step(7)
    step(8)
    attended(*steps[5])
    wo_load.wait()
    for m in wo_sib:
        m.wait_recv()
    attended(*steps[6])
    attended(*steps[7])
    project_out(0)
    attended(*steps[8])
    project_out(1)
    project_out(2)
    for c in range(CH):
        finish(c)
    for copy in sent:
        copy.wait_send()


MESSAGES = 7 + 6 + 12 + 30 + 54 + 27 - 3 * len(DIRECT) + 27 + 3


def per_device(tokens, survive, norm_gain, w_qkv, qk_gain, w_out):
    vmem = lambda *shape: pltpu.VMEM(shape, bf16)
    vmem32 = lambda *shape: pltpu.VMEM(shape, f32)
    units = (HEADS, CH)
    scratch = [
        vmem(POS, WIDTH), vmem(POS, WIDTH), vmem(3, WIDTH, POS), vmem(4, POS, 2 * POS),
        vmem(4, HEADS, POS, D), vmem(HEADS, 8, POS, 2 * D), vmem32(8, 8, 128), vmem(8, POS, D),
        vmem32(*units, RC, D), vmem32(*units, 4, RC, D),
        vmem(*units, 3, RC, D), vmem(*units, HALF, D), vmem(*units, HALF, D),
        vmem(*units, RC, D), vmem(*units, RC, D), vmem(len(DIRECT), RC, D), vmem(*units, 2, HALF, D),
        vmem32(*units, 3, 1, RC), vmem32(*units, 1, RC), vmem32(*units, 1, RC), vmem32(*units, 1, RC),
        vmem32(len(DIRECT), 1, RC), vmem32(*units, 1, RC),
        vmem(4, *units, RC, D), vmem32(CH, RC, POS), vmem(CH, RC, POS), vmem(CH, RC, POS),
        pltpu.SemaphoreType.DMA((CH + 4,)),
        pltpu.SemaphoreType.DMA((MESSAGES,)),
        pltpu.SemaphoreType.DMA((MESSAGES,)),
    ]
    in_hbm = pl.BlockSpec(memory_space=pl.ANY)
    in_vmem = pl.BlockSpec(memory_space=pltpu.VMEM)
    share = pl.pallas_call(
        kernel,
        out_shape=jax.ShapeDtypeStruct((POS, POS), bf16),
        in_specs=[in_hbm, in_vmem, in_vmem, in_hbm, in_vmem, in_hbm],
        out_specs=in_vmem,
        scratch_shapes=scratch,
        compiler_params=pltpu.CompilerParams(
            collective_id=0, has_side_effects=True, vmem_limit_bytes=60 * 2**20
        ),
        name="branch",
    )(
        tokens,
        survive.reshape(CH, RC),
        norm_gain.reshape(1, WIDTH),
        jnp.transpose(w_qkv, (1, 0, 2)),
        jnp.transpose(qk_gain, (1, 0, 2)),
        w_out,
    )
    return jnp.where(survive[:, None] == 1, share, jnp.zeros_like(share))


def solution(mesh):
    placed = (
        P("seq", None),
        P("seq"),
        P(),
        P(None, None, "head"),
        P(None, "head", None),
        P("head", None),
    )
    return jax.shard_map(
        per_device, mesh=mesh, in_specs=placed, out_specs=P("seq", "head"), check_vma=False
    )
```

```python
import math

import jax
import jax.numpy as jnp
from jax import lax
from jax.experimental import pallas as pl
from jax.experimental.pallas import tpu as pltpu
from jax.sharding import PartitionSpec as P

epsilon = 1e-06
MESH = pl.DeviceIdType.MESH
f32, bf16 = jnp.float32, jnp.bfloat16

POS = 384
WIDTH = 3072
HEADS = 3
D = 128
CH = 3
RC = POS // CH
HALF = RC // 2
DIRECT = [(2, 0), (2, 1), (2, 2)]


def column_of(row):
    return jnp.transpose(jnp.broadcast_to(row, (128, 128)))


def head_norm(x, gain):
    center = x - jnp.mean(x, axis=-1, keepdims=True)
    spread = jnp.mean(center * center, axis=-1, keepdims=True)
    return center * lax.rsqrt(spread + epsilon) * gain


def kernel(
    tok_hbm, sv_ref, ng_ref, w_hbm, qg_ref, wo_hbm, out_ref,
    tok, normed, w, wo, q, kv, lrow, lv, own, dn,
    zs, zra, zrb, zfm, zfp, zff, zt, ds, dra, dfm, dfp, dff, dt,
    xa, total, zls, zlr,
    lsem, ssem, rsem,
):
    s = lax.axis_index("seq")
    hd = lax.axis_index("head")
    y, zh, co = s // 8, (s // 2) % 4, s % 2
    x, zl = hd // 2, hd % 2

    def seq_at(dy, dz, flip):
        c = (1 - co) if flip else co
        return {"seq": (((y + dy) % 4) * 4 + (zh + dz) % 4) * 2 + c}

    y_next, y_prev, sib = seq_at(1, 0, False), seq_at(3, 0, False), seq_at(0, 0, True)
    z_next, z_prev, z_far = (seq_at(0, dz, False) for dz in (1, 3, 2))
    x_next, x_prev, x_far = ({"head": ((x + dx) % 4) * 2 + zl} for dx in (1, 3, 2))
    z_pair = {"head": x * 2 + (1 - zl)}
    line = [
        (sib, 1), (y_next, 2), (seq_at(1, 0, True), 3), (y_prev, 4),
        (seq_at(3, 0, True), 5), (seq_at(2, 0, False), 6), (seq_at(2, 0, True), 7),
    ]

    token_loads = []
    for c in range(CH):
        rows = pl.ds(c * RC, RC)
        token_loads.append(pltpu.make_async_copy(tok_hbm.at[rows], tok.at[rows], lsem.at[c]))
    w_loads = [pltpu.make_async_copy(w_hbm.at[j], w.at[j], lsem.at[CH + j]) for j in range(3)]
    x_cols = lambda dx: pl.ds(pl.multiple_of(((x + dx) % 4) * 2 * POS, 128), 2 * POS)
    wo_load = pltpu.make_async_copy(wo_hbm.at[:, x_cols(0)], wo.at[0], lsem.at[CH + 3])
    for load in token_loads + w_loads[0:1]:
        load.start()

    barrier = pltpu.get_barrier_semaphore()
    peers = [p for p, _ in line] + [z_next, z_prev, z_far, x_next, x_prev, x_far, z_pair]
    for peer in peers:
        pl.semaphore_signal(barrier, inc=1, device_id=peer, device_id_type=MESH)

    count = [0]
    sent = []

    def message(src, dst, peer):
        i = count[0]
        count[0] += 1
        copy = pltpu.make_async_remote_copy(
            src_ref=src, dst_ref=dst, send_sem=ssem.at[i], recv_sem=rsem.at[i],
            device_id=peer, device_id_type=MESH,
        )
        sent.append(copy)
        return copy

    lrow[0] = jnp.zeros((8, 128), f32)
    lrow[0, 0:CH, :] = (sv_ref[...] == 1).astype(f32)

    def spread_live(slot):
        for t in range(CH):
            lv[slot, t * RC : (t + 1) * RC, :] = column_of(lrow[slot, t : t + 1, :]).astype(bf16)

    def norm_rows(i, carry):
        rows = pl.ds(pl.multiple_of(i * 32, 32), 32)
        v = tok[rows, :].astype(f32)
        center = v - jnp.mean(v, axis=-1, keepdims=True)
        spread = jnp.mean(center * center, axis=-1, keepdims=True)
        normed[rows, :] = (center * lax.rsqrt(spread + epsilon) * ng_ref[...]).astype(bf16)
        return carry

    score_scale = math.log2(math.e) / math.sqrt(D)
    lo, hi = pl.ds(0, POS // 2), pl.ds(POS // 2, POS // 2)
    q_next, q_prev, q_fwd_next, q_fwd_prev = [], [], [], []
    for c in range(CH):
        rows = pl.ds(c * RC, RC)
        first, second = pl.ds(c * RC, HALF), pl.ds(c * RC + HALF, HALF)
        q_next.append(message(q.at[0, :, rows], q.at[1, :, rows], z_next))
        q_prev.append(message(q.at[0, :, rows], q.at[2, :, rows], z_prev))
        q_fwd_next.append(message(q.at[1, :, first], q.at[3, :, first], z_next))
        q_fwd_prev.append(message(q.at[2, :, second], q.at[3, :, second], z_prev))

    for c in range(CH):
        token_loads[c].wait()
        if c == CH - 1:
            for load in w_loads[1:] + [wo_load]:
                load.start()
        lax.fori_loop(c * RC // 32, (c + 1) * RC // 32, norm_rows, 0)
        if c == 0:
            w_loads[0].wait()
        rows = slice(c * RC, (c + 1) * RC)
        projected = jnp.dot(normed[rows, :], w[0], preferred_element_type=f32)
        for h in range(HEADS):
            gain = qg_ref[h, 0:1, :] * score_scale
            q[0, h, rows, :] = head_norm(projected[:, h * D : (h + 1) * D], gain).astype(bf16)
        if c == 0:
            pl.semaphore_wait(barrier, len(peers))
        if c < CH - 1:
            q_next[c].start()
            q_prev[c].start()

    live_msg = [message(lrow.at[0], lrow.at[slot], peer) for peer, slot in line]
    core_rows = pl.ds(pl.multiple_of(co * (POS // 2), 16), POS // 2)
    wo_msg = [
        message(wo_hbm.at[core_rows, x_cols(dx)], wo.at[r, core_rows], peer)
        for dx, r, peer in ((1, 1, x_next), (3, 2, x_prev), (2, 3, x_far))
    ]
    wo_sib = [message(wo.at[r, core_rows], wo.at[r, core_rows], sib) for r in (1, 2, 3)]

    kv_next = [[message(kv.at[h, 0, half], kv.at[h, 2, half], y_next) for half in (lo, hi)] for h in range(HEADS)]
    kv_prev = [[message(kv.at[h, 0, half], kv.at[h, 4, half], y_prev) for half in (hi, lo)] for h in range(HEADS)]
    kv_fwd_next = [message(kv.at[h, 2, lo], kv.at[h, 6, lo], y_next) for h in range(HEADS)]
    kv_fwd_prev = [message(kv.at[h, 4, hi], kv.at[h, 6, hi], y_prev) for h in range(HEADS)]
    kv_sib = [[message(kv.at[h, 2 * r], kv.at[h, 2 * r + 1], sib) for r in range(4)] for h in range(HEADS)]

    def send_kv(h, part):
        kv_next[h][part].start()
        kv_prev[h][part].start()

    def forward_q(c):
        q_next[c].wait_recv()
        q_fwd_next[c].start()
        q_prev[c].wait_recv()
        q_fwd_prev[c].start()

    def forward_kv(h):
        kv_next[h][0].wait_recv()
        kv_fwd_next[h].start()
        kv_prev[h][0].wait_recv()
        kv_fwd_prev[h].start()

    def share_near(h):
        kv_next[h][1].wait_recv()
        kv_sib[h][1].start()
        kv_prev[h][1].wait_recv()
        kv_sib[h][2].start()

    def share_far(h):
        kv_fwd_next[h].wait_recv()
        kv_fwd_prev[h].wait_recv()
        kv_sib[h][3].start()

    def queries_in(c):
        q_fwd_next[c].wait_recv()
        q_fwd_prev[c].wait_recv()

    def all_in(h):
        for m in kv_sib[h]:
            m.wait_recv()

    def project_kv(h):
        cols = pl.ds(h * D, D)
        weights = jnp.concatenate([w[1, :, cols], w[2, :, cols]], axis=1)
        projected = jnp.dot(normed[...], weights, preferred_element_type=f32)
        kv[h, 0, :, 0:D] = head_norm(projected[:, :D], qg_ref[h, 1:2, :]).astype(bf16)
        kv[h, 0, :, D:] = (projected[:, D:] * lv[0].astype(f32)).astype(bf16)

    for m in live_msg + wo_msg:
        m.start()
    spread_live(0)
    w_loads[1].wait()
    w_loads[2].wait()
    project_kv(0)
    send_kv(0, 0)
    send_kv(0, 1)
    kv_sib[0][0].start()
    project_kv(1)
    send_kv(1, 0)
    kv_sib[1][0].start()
    forward_q(0)
    q_next[2].start()
    q_prev[2].start()
    project_kv(2)
    kv_sib[2][0].start()
    for m, (_, slot) in zip(live_msg[:3], line[:3]):
        m.wait_recv()
        spread_live(slot)
    forward_kv(0)
    send_kv(1, 1)
    send_kv(2, 0)
    for m, (_, slot) in zip(live_msg[3:], line[3:]):
        m.wait_recv()
        spread_live(slot)

    def unit(h, c):
        rows = pl.ds(c * RC, RC)
        queries = jnp.concatenate([q[slot, h, rows, :] for slot in range(4)], axis=0)
        keys = kv[h, :, :, 0:D].reshape(8 * POS, D)
        scores = lax.dot_general(queries, keys, (((1,), (1,)), ((), ())), preferred_element_type=f32)
        weights = jnp.exp2(scores).astype(bf16)
        values = jnp.concatenate([kv[h, :, :, D:].reshape(8 * POS, D), lv[...].reshape(8 * POS, D)], axis=1)
        acc = jnp.dot(weights, values, preferred_element_type=f32)
        own[h, c] = acc[0:RC, 0:D]
        for slot in range(1, 4):
            zs[h, c, slot - 1] = acc[slot * RC : (slot + 1) * RC, 0:D].astype(bf16)
        for slot in range(4):
            dn[h, c, slot] = acc[slot * RC : (slot + 1) * RC, D:]

    A, B = pl.ds(0, HALF), pl.ds(HALF, HALF)
    zmsg, dmsg = {}, {}
    for h in range(HEADS):
        for c in range(CH):
            if (h, c) in DIRECT:
                i = DIRECT.index((h, c))
                zmsg[h, c] = [
                    message(zs.at[h, c, 2], zff.at[i], z_far),
                    message(zs.at[h, c, 1], zfm.at[h, c], z_next),
                    message(zs.at[h, c, 0], zfp.at[h, c], z_prev),
                ]
                dmsg[h, c] = [
                    message(ds.at[h, c, 2], dff.at[i], z_far),
                    message(ds.at[h, c, 1], dfm.at[h, c], z_next),
                    message(ds.at[h, c, 0], dfp.at[h, c], z_prev),
                ]
                continue
            zmsg[h, c] = [
                message(zs.at[h, c, 2, A], zra.at[h, c], z_next),
                message(zs.at[h, c, 2, B], zrb.at[h, c], z_prev),
                message(zs.at[h, c, 1, B], zfm.at[h, c, B], z_next),
                message(zs.at[h, c, 0, A], zfp.at[h, c, A], z_prev),
                message(zt.at[h, c, 0], zfm.at[h, c, A], z_next),
                message(zt.at[h, c, 1], zfp.at[h, c, B], z_prev),
            ]
            dmsg[h, c] = [
                message(ds.at[h, c, 2], dra.at[h, c], z_next),
                message(ds.at[h, c, 0], dfp.at[h, c], z_prev),
                message(dt.at[h, c], dfm.at[h, c], z_next),
            ]

    def z_first(h, c):
        for m in zmsg[h, c][:4]:
            m.start()
        lane = lax.broadcasted_iota(jnp.int32, (RC, D), 1)
        mixed = jnp.where(lane == 0, dn[h, c, 1], jnp.where(lane == 1, dn[h, c, 2], dn[h, c, 3]))
        rows = jnp.transpose(mixed)[0:8, :]
        for i in range(3):
            ds[h, c, i] = rows[i : i + 1, :]
        for d in dmsg[h, c] if (h, c) in DIRECT else dmsg[h, c][:2]:
            d.start()

    def z_relay(h, c):
        if (h, c) in DIRECT:
            return
        m = zmsg[h, c]
        m[0].wait_recv()
        zt[h, c, 0] = (zra[h, c].astype(f32) + zs[h, c, 1, 0:HALF].astype(f32)).astype(bf16)
        m[4].start()
        m[1].wait_recv()
        zt[h, c, 1] = (zrb[h, c].astype(f32) + zs[h, c, 0, HALF:].astype(f32)).astype(bf16)
        m[5].start()
        d = dmsg[h, c]
        d[0].wait_recv()
        dt[h, c] = dra[h, c] + ds[h, c, 1]
        d[2].start()

    xmsg = {}
    for h in range(HEADS):
        for c in range(CH):
            xmsg[h, c] = [
                message(xa.at[0, h, c], xa.at[r, h, c], peer)
                for r, peer in ((3, x_far), (1, x_next), (2, x_prev))
            ]
    zlmsg = [message(zls.at[c], zlr.at[c], z_pair) for c in range(CH)]

    def attended(h, c):
        direct = (h, c) in DIRECT
        for m in dmsg[h, c][0 if direct else 1 :] + zmsg[h, c][0 if direct else 2 :]:
            m.wait_recv()
        others = dfm[h, c] + dfp[h, c]
        num = own[h, c] + zfm[h, c].astype(f32) + zfp[h, c].astype(f32)
        if direct:
            others = others + dff[DIRECT.index((h, c))]
            num = num + zff[DIRECT.index((h, c))].astype(f32)
        den = dn[h, c, 0] + column_of(others)
        xa[0, h, c] = (num / den).astype(bf16)
        for m in xmsg[h, c]:
            m.start()

    def project_out(c):
        for h in range(HEADS):
            for m in xmsg[h, c]:
                m.wait_recv()
        rows = jnp.concatenate([xa[r, h, c] for r in range(4) for h in range(HEADS)], axis=1)
        other = pl.ds(pl.multiple_of((1 - zl) * POS, 128), POS)
        mine = pl.ds(pl.multiple_of(zl * POS, 128), POS)
        theirs = wo[:, :, other].reshape(4 * POS, POS)
        zls[c] = jnp.dot(rows, theirs, preferred_element_type=f32).astype(bf16)
        zlmsg[c].start()
        total[c] = jnp.dot(rows, wo[:, :, mine].reshape(4 * POS, POS), preferred_element_type=f32)

    def finish(c):
        zlmsg[c].wait_recv()
        out_ref[c * RC : (c + 1) * RC, :] = (total[c] + zlr[c].astype(f32)).astype(bf16)

    def share_weights():
        for m, share in zip(wo_msg, wo_sib):
            m.wait_recv()
            share.start()

    steps = [(h, c) for h in range(HEADS) for c in range(CH)]

    def after(u):
        z_first(*steps[u])
        if u >= 2:
            z_relay(*steps[u - 2])

    def step(u):
        unit(*steps[u])
        after(u)

    share_near(0)
    forward_q(1)
    forward_kv(1)
    send_kv(2, 1)
    share_far(0)
    queries_in(0)
    all_in(0)
    step(0)
    forward_q(2)
    share_near(1)
    forward_kv(2)
    queries_in(1)
    step(1)
    share_far(1)
    share_near(2)
    queries_in(2)
    step(2)
    all_in(1)
    share_far(2)
    step(3)
    step(4)
    share_weights()
    step(5)
    all_in(2)
    step(6)
    step(7)
    step(8)
    for u in range(6):
        attended(*steps[u])
    wo_load.wait()
    for m in wo_sib:
        m.wait_recv()
    attended(*steps[6])
    attended(*steps[7])
    project_out(0)
    attended(*steps[8])
    project_out(1)
    project_out(2)
    for c in range(CH):
        finish(c)
    for copy in sent:
        copy.wait_send()


MESSAGES = 7 + 6 + 12 + 30 + 54 + 27 - 3 * len(DIRECT) + 27 + 3


def per_device(tokens, survive, norm_gain, w_qkv, qk_gain, w_out):
    vmem = lambda *shape: pltpu.VMEM(shape, bf16)
    vmem32 = lambda *shape: pltpu.VMEM(shape, f32)
    units = (HEADS, CH)
    scratch = [
        vmem(POS, WIDTH), vmem(POS, WIDTH), vmem(3, WIDTH, POS), vmem(4, POS, 2 * POS),
        vmem(4, HEADS, POS, D), vmem(HEADS, 8, POS, 2 * D), vmem32(8, 8, 128), vmem(8, POS, D),
        vmem32(*units, RC, D), vmem32(*units, 4, RC, D),
        vmem(*units, 3, RC, D), vmem(*units, HALF, D), vmem(*units, HALF, D),
        vmem(*units, RC, D), vmem(*units, RC, D), vmem(len(DIRECT), RC, D), vmem(*units, 2, HALF, D),
        vmem32(*units, 3, 1, RC), vmem32(*units, 1, RC), vmem32(*units, 1, RC), vmem32(*units, 1, RC),
        vmem32(len(DIRECT), 1, RC), vmem32(*units, 1, RC),
        vmem(4, *units, RC, D), vmem32(CH, RC, POS), vmem(CH, RC, POS), vmem(CH, RC, POS),
        pltpu.SemaphoreType.DMA((CH + 4,)),
        pltpu.SemaphoreType.DMA((MESSAGES,)),
        pltpu.SemaphoreType.DMA((MESSAGES,)),
    ]
    in_hbm = pl.BlockSpec(memory_space=pl.ANY)
    in_vmem = pl.BlockSpec(memory_space=pltpu.VMEM)
    share = pl.pallas_call(
        kernel,
        out_shape=jax.ShapeDtypeStruct((POS, POS), bf16),
        in_specs=[in_hbm, in_vmem, in_vmem, in_hbm, in_vmem, in_hbm],
        out_specs=in_vmem,
        scratch_shapes=scratch,
        compiler_params=pltpu.CompilerParams(
            collective_id=0, has_side_effects=True, vmem_limit_bytes=60 * 2**20
        ),
        name="branch",
    )(
        tokens,
        survive.reshape(CH, RC),
        norm_gain.reshape(1, WIDTH),
        jnp.transpose(w_qkv, (1, 0, 2)),
        jnp.transpose(qk_gain, (1, 0, 2)),
        w_out,
    )
    return jnp.where(survive[:, None] == 1, share, jnp.zeros_like(share))


def solution(mesh):
    placed = (
        P("seq", None),
        P("seq"),
        P(),
        P(None, None, "head"),
        P(None, "head", None),
        P("head", None),
    )
    return jax.shard_map(
        per_device, mesh=mesh, in_specs=placed, out_specs=P("seq", "head"), check_vma=False
    )
```

```python
import math

import jax
import jax.numpy as jnp
from jax import lax
from jax.experimental import pallas as pl
from jax.experimental.pallas import tpu as pltpu
from jax.sharding import PartitionSpec as P

epsilon = 1e-06
MESH = pl.DeviceIdType.MESH
f32, bf16 = jnp.float32, jnp.bfloat16

POS = 384
WIDTH = 3072
HEADS = 3
D = 128
CH = 3
RC = POS // CH
HALF = RC // 2
DIRECT = [(2, 0), (2, 1), (2, 2)]


def column_of(row):
    return jnp.transpose(jnp.broadcast_to(row, (128, 128)))


def head_norm(x, gain):
    center = x - jnp.mean(x, axis=-1, keepdims=True)
    spread = jnp.mean(center * center, axis=-1, keepdims=True)
    return center * lax.rsqrt(spread + epsilon) * gain


def kernel(
    tok_hbm, sv_ref, ng_ref, w_hbm, qg_ref, wo_hbm, out_ref,
    tok, normed, w, wo, q, kv, lrow, lv, own, dn,
    zs, zra, zrb, zfm, zfp, zff, zt, ds, dra, dfm, dfp, dff, dt,
    xa, total, zls, zlr,
    lsem, ssem, rsem,
):
    s = lax.axis_index("seq")
    hd = lax.axis_index("head")
    y, zh, co = s // 8, (s // 2) % 4, s % 2
    x, zl = hd // 2, hd % 2

    def seq_at(dy, dz, flip):
        c = (1 - co) if flip else co
        return {"seq": (((y + dy) % 4) * 4 + (zh + dz) % 4) * 2 + c}

    y_next, y_prev, sib = seq_at(1, 0, False), seq_at(3, 0, False), seq_at(0, 0, True)
    z_next, z_prev, z_far = (seq_at(0, dz, False) for dz in (1, 3, 2))
    x_next, x_prev, x_far = ({"head": ((x + dx) % 4) * 2 + zl} for dx in (1, 3, 2))
    z_pair = {"head": x * 2 + (1 - zl)}
    line = [
        (sib, 1), (y_next, 2), (seq_at(1, 0, True), 3), (y_prev, 4),
        (seq_at(3, 0, True), 5), (seq_at(2, 0, False), 6), (seq_at(2, 0, True), 7),
    ]

    token_loads = []
    for c in range(CH):
        rows = pl.ds(c * RC, RC)
        token_loads.append(pltpu.make_async_copy(tok_hbm.at[rows], tok.at[rows], lsem.at[c]))
    w_loads = [pltpu.make_async_copy(w_hbm.at[j], w.at[j], lsem.at[CH + j]) for j in range(3)]
    x_cols = lambda dx: pl.ds(pl.multiple_of(((x + dx) % 4) * 2 * POS, 128), 2 * POS)
    wo_load = pltpu.make_async_copy(wo_hbm.at[:, x_cols(0)], wo.at[0], lsem.at[CH + 3])
    for load in token_loads + w_loads[0:1]:
        load.start()

    barrier = pltpu.get_barrier_semaphore()
    peers = [p for p, _ in line] + [z_next, z_prev, z_far, x_next, x_prev, x_far, z_pair]
    for peer in peers:
        pl.semaphore_signal(barrier, inc=1, device_id=peer, device_id_type=MESH)

    count = [0]
    sent = []

    def message(src, dst, peer):
        i = count[0]
        count[0] += 1
        copy = pltpu.make_async_remote_copy(
            src_ref=src, dst_ref=dst, send_sem=ssem.at[i], recv_sem=rsem.at[i],
            device_id=peer, device_id_type=MESH,
        )
        sent.append(copy)
        return copy

    lrow[0] = jnp.zeros((8, 128), f32)
    lrow[0, 0:CH, :] = (sv_ref[...] == 1).astype(f32)

    def spread_live(slot):
        for t in range(CH):
            lv[slot, t * RC : (t + 1) * RC, :] = column_of(lrow[slot, t : t + 1, :]).astype(bf16)

    def norm_rows(i, carry):
        rows = pl.ds(pl.multiple_of(i * 32, 32), 32)
        v = tok[rows, :].astype(f32)
        center = v - jnp.mean(v, axis=-1, keepdims=True)
        spread = jnp.mean(center * center, axis=-1, keepdims=True)
        normed[rows, :] = (center * lax.rsqrt(spread + epsilon) * ng_ref[...]).astype(bf16)
        return carry

    score_scale = math.log2(math.e) / math.sqrt(D)
    lo, hi = pl.ds(0, POS // 2), pl.ds(POS // 2, POS // 2)
    q_next, q_prev, q_fwd_next, q_fwd_prev = [], [], [], []
    for c in range(CH):
        rows = pl.ds(c * RC, RC)
        first, second = pl.ds(c * RC, HALF), pl.ds(c * RC + HALF, HALF)
        q_next.append(message(q.at[0, :, rows], q.at[1, :, rows], z_next))
        q_prev.append(message(q.at[0, :, rows], q.at[2, :, rows], z_prev))
        q_fwd_next.append(message(q.at[1, :, first], q.at[3, :, first], z_next))
        q_fwd_prev.append(message(q.at[2, :, second], q.at[3, :, second], z_prev))

    def project_q(c):
        rows = slice(c * RC, (c + 1) * RC)
        projected = jnp.dot(normed[rows, :], w[0], preferred_element_type=f32)
        for h in range(HEADS):
            gain = qg_ref[h, 0:1, :] * score_scale
            q[0, h, rows, :] = head_norm(projected[:, h * D : (h + 1) * D], gain).astype(bf16)

    def send_q(c):
        q_next[c].start()
        q_prev[c].start()

    for c in range(CH):
        token_loads[c].wait()
        if c == 1:
            for load in w_loads[1:] + [wo_load]:
                load.start()
        lax.fori_loop(c * RC // 32, (c + 1) * RC // 32, norm_rows, 0)
        if c == 0:
            w_loads[0].wait()
            project_q(0)
            pl.semaphore_wait(barrier, len(peers))
            send_q(0)

    live_msg = [message(lrow.at[0], lrow.at[slot], peer) for peer, slot in line]
    core_rows = pl.ds(pl.multiple_of(co * (POS // 2), 16), POS // 2)
    wo_msg = [
        message(wo_hbm.at[core_rows, x_cols(dx)], wo.at[r, core_rows], peer)
        for dx, r, peer in ((1, 1, x_next), (3, 2, x_prev), (2, 3, x_far))
    ]
    wo_sib = [message(wo.at[r, core_rows], wo.at[r, core_rows], sib) for r in (1, 2, 3)]

    kv_next = [[message(kv.at[h, 0, half], kv.at[h, 2, half], y_next) for half in (lo, hi)] for h in range(HEADS)]
    kv_prev = [[message(kv.at[h, 0, half], kv.at[h, 4, half], y_prev) for half in (hi, lo)] for h in range(HEADS)]
    kv_fwd_next = [message(kv.at[h, 2, lo], kv.at[h, 6, lo], y_next) for h in range(HEADS)]
    kv_fwd_prev = [message(kv.at[h, 4, hi], kv.at[h, 6, hi], y_prev) for h in range(HEADS)]
    kv_sib = [[message(kv.at[h, 2 * r], kv.at[h, 2 * r + 1], sib) for r in range(4)] for h in range(HEADS)]

    def send_kv(h, part):
        kv_next[h][part].start()
        kv_prev[h][part].start()

    def forward_q(c):
        q_next[c].wait_recv()
        q_fwd_next[c].start()
        q_prev[c].wait_recv()
        q_fwd_prev[c].start()

    def forward_kv(h):
        kv_next[h][0].wait_recv()
        kv_fwd_next[h].start()
        kv_prev[h][0].wait_recv()
        kv_fwd_prev[h].start()

    def share_near(h):
        kv_next[h][1].wait_recv()
        kv_sib[h][1].start()
        kv_prev[h][1].wait_recv()
        kv_sib[h][2].start()

    def share_far(h):
        kv_fwd_next[h].wait_recv()
        kv_fwd_prev[h].wait_recv()
        kv_sib[h][3].start()

    def queries_in(c):
        q_fwd_next[c].wait_recv()
        q_fwd_prev[c].wait_recv()

    def all_in(h):
        for m in kv_sib[h]:
            m.wait_recv()

    def project_kv(h):
        cols = pl.ds(h * D, D)
        weights = jnp.concatenate([w[1, :, cols], w[2, :, cols]], axis=1)
        projected = jnp.dot(normed[...], weights, preferred_element_type=f32)
        kv[h, 0, :, 0:D] = head_norm(projected[:, :D], qg_ref[h, 1:2, :]).astype(bf16)
        kv[h, 0, :, D:] = (projected[:, D:] * lv[0].astype(f32)).astype(bf16)

    for m in live_msg + wo_msg:
        m.start()
    spread_live(0)
    w_loads[1].wait()
    w_loads[2].wait()
    project_kv(0)
    send_kv(0, 0)
    send_kv(0, 1)
    kv_sib[0][0].start()
    project_q(1)
    send_q(1)
    project_q(2)
    project_kv(1)
    send_kv(1, 0)
    kv_sib[1][0].start()
    forward_q(0)
    send_q(2)
    project_kv(2)
    kv_sib[2][0].start()
    for m, (_, slot) in zip(live_msg[:3], line[:3]):
        m.wait_recv()
        spread_live(slot)
    forward_kv(0)
    send_kv(1, 1)
    send_kv(2, 0)
    for m, (_, slot) in zip(live_msg[3:], line[3:]):
        m.wait_recv()
        spread_live(slot)

    def attend(queries, h):
        keys = kv[h, :, :, 0:D].reshape(8 * POS, D)
        scores = lax.dot_general(queries, keys, (((1,), (1,)), ((), ())), preferred_element_type=f32)
        weights = jnp.exp2(scores).astype(bf16)
        values = jnp.concatenate([kv[h, :, :, D:].reshape(8 * POS, D), lv[...].reshape(8 * POS, D)], axis=1)
        return jnp.dot(weights, values, preferred_element_type=f32)

    def keep(acc, h, c, slot):
        if slot == 0:
            own[h, c] = acc[:, 0:D]
        else:
            zs[h, c, slot - 1] = acc[:, 0:D].astype(bf16)
        dn[h, c, slot] = acc[:, D:]

    def unit(h, c, slots):
        acc = attend(jnp.concatenate([q[slot, h, c * RC : (c + 1) * RC, :] for slot in slots], axis=0), h)
        for i, slot in enumerate(slots):
            keep(acc[i * RC : (i + 1) * RC], h, c, slot)

    def far_unit(h):
        acc = attend(q[3, h], h)
        for c in range(CH):
            keep(acc[c * RC : (c + 1) * RC], h, c, 3)

    A, B = pl.ds(0, HALF), pl.ds(HALF, HALF)
    zmsg, dmsg = {}, {}
    for h in range(HEADS):
        for c in range(CH):
            if (h, c) in DIRECT:
                i = DIRECT.index((h, c))
                zmsg[h, c] = [
                    message(zs.at[h, c, 2], zff.at[i], z_far),
                    message(zs.at[h, c, 1], zfm.at[h, c], z_next),
                    message(zs.at[h, c, 0], zfp.at[h, c], z_prev),
                ]
                dmsg[h, c] = [
                    message(ds.at[h, c, 2], dff.at[i], z_far),
                    message(ds.at[h, c, 1], dfm.at[h, c], z_next),
                    message(ds.at[h, c, 0], dfp.at[h, c], z_prev),
                ]
                continue
            zmsg[h, c] = [
                message(zs.at[h, c, 2, A], zra.at[h, c], z_next),
                message(zs.at[h, c, 2, B], zrb.at[h, c], z_prev),
                message(zs.at[h, c, 1, B], zfm.at[h, c, B], z_next),
                message(zs.at[h, c, 0, A], zfp.at[h, c, A], z_prev),
                message(zt.at[h, c, 0], zfm.at[h, c, A], z_next),
                message(zt.at[h, c, 1], zfp.at[h, c, B], z_prev),
            ]
            dmsg[h, c] = [
                message(ds.at[h, c, 2], dra.at[h, c], z_next),
                message(ds.at[h, c, 0], dfp.at[h, c], z_prev),
                message(dt.at[h, c], dfm.at[h, c], z_next),
            ]

    def z_near(h, c):
        for m in zmsg[h, c][2:4]:
            m.start()

    def z_first(h, c, sends):
        for m in zmsg[h, c][sends]:
            m.start()
        lane = lax.broadcasted_iota(jnp.int32, (RC, D), 1)
        mixed = jnp.where(lane == 0, dn[h, c, 1], jnp.where(lane == 1, dn[h, c, 2], dn[h, c, 3]))
        rows = jnp.transpose(mixed)[0:8, :]
        for i in range(3):
            ds[h, c, i] = rows[i : i + 1, :]
        for d in dmsg[h, c] if (h, c) in DIRECT else dmsg[h, c][:2]:
            d.start()

    def z_relay(h, c):
        if (h, c) in DIRECT:
            return
        m = zmsg[h, c]
        m[0].wait_recv()
        zt[h, c, 0] = (zra[h, c].astype(f32) + zs[h, c, 1, 0:HALF].astype(f32)).astype(bf16)
        m[4].start()
        m[1].wait_recv()
        zt[h, c, 1] = (zrb[h, c].astype(f32) + zs[h, c, 0, HALF:].astype(f32)).astype(bf16)
        m[5].start()
        d = dmsg[h, c]
        d[0].wait_recv()
        dt[h, c] = dra[h, c] + ds[h, c, 1]
        d[2].start()

    xmsg = {}
    for h in range(HEADS):
        for c in range(CH):
            xmsg[h, c] = [
                message(xa.at[0, h, c], xa.at[r, h, c], peer)
                for r, peer in ((3, x_far), (1, x_next), (2, x_prev))
            ]
    zlmsg = [message(zls.at[c], zlr.at[c], z_pair) for c in range(CH)]

    def attended(h, c):
        direct = (h, c) in DIRECT
        for m in dmsg[h, c][0 if direct else 1 :] + zmsg[h, c][0 if direct else 2 :]:
            m.wait_recv()
        others = dfm[h, c] + dfp[h, c]
        num = own[h, c] + zfm[h, c].astype(f32) + zfp[h, c].astype(f32)
        if direct:
            others = others + dff[DIRECT.index((h, c))]
            num = num + zff[DIRECT.index((h, c))].astype(f32)
        den = dn[h, c, 0] + column_of(others)
        xa[0, h, c] = (num / den).astype(bf16)
        for m in xmsg[h, c]:
            m.start()

    def project_out(c):
        for h in range(HEADS):
            for m in xmsg[h, c]:
                m.wait_recv()
        rows = jnp.concatenate([xa[r, h, c] for r in range(4) for h in range(HEADS)], axis=1)
        other = pl.ds(pl.multiple_of((1 - zl) * POS, 128), POS)
        mine = pl.ds(pl.multiple_of(zl * POS, 128), POS)
        theirs = wo[:, :, other].reshape(4 * POS, POS)
        zls[c] = jnp.dot(rows, theirs, preferred_element_type=f32).astype(bf16)
        zlmsg[c].start()
        total[c] = jnp.dot(rows, wo[:, :, mine].reshape(4 * POS, POS), preferred_element_type=f32)

    def finish(c):
        zlmsg[c].wait_recv()
        mask = jnp.concatenate([lv[0, c * RC : (c + 1) * RC, :].astype(f32)] * (POS // D), axis=1)
        share = jnp.where(mask > 0.5, total[c] + zlr[c].astype(f32), 0.0)
        out_ref[c * RC : (c + 1) * RC, :] = share.astype(bf16)

    def share_weights():
        for m, share in zip(wo_msg, wo_sib):
            m.wait_recv()
            share.start()

    steps = [(h, c) for h in range(HEADS) for c in range(CH)]

    def step(u):
        unit(*steps[u], range(4))
        z_first(*steps[u], slice(0, 4))

    share_near(0)
    forward_q(1)
    forward_kv(1)
    send_kv(2, 1)
    share_far(0)
    all_in(0)
    unit(0, 0, range(3))
    z_near(0, 0)
    forward_q(2)
    share_near(1)
    forward_kv(2)
    unit(0, 1, range(3))
    z_near(0, 1)
    share_far(1)
    unit(0, 2, range(3))
    z_near(0, 2)
    share_near(2)
    for c in range(CH):
        queries_in(c)
    far_unit(0)
    for c in range(CH):
        z_first(0, c, slice(0, 2))
    all_in(1)
    step(3)
    share_far(2)
    step(4)
    z_relay(0, 0)
    z_relay(0, 1)
    share_weights()
    step(5)
    z_relay(0, 2)
    z_relay(1, 0)
    all_in(2)
    step(6)
    z_relay(1, 1)
    step(7)
    z_relay(1, 2)
    step(8)
    for u in range(6):
        attended(*steps[u])
    wo_load.wait()
    for m in wo_sib:
        m.wait_recv()
    attended(*steps[6])
    attended(*steps[7])
    project_out(0)
    attended(*steps[8])
    project_out(1)
    project_out(2)
    for c in range(CH):
        finish(c)
    for copy in sent:
        copy.wait_send()


MESSAGES = 7 + 6 + 12 + 30 + 54 + 27 - 3 * len(DIRECT) + 27 + 3


def per_device(tokens, survive, norm_gain, w_qkv, qk_gain, w_out):
    vmem = lambda *shape: pltpu.VMEM(shape, bf16)
    vmem32 = lambda *shape: pltpu.VMEM(shape, f32)
    units = (HEADS, CH)
    scratch = [
        vmem(POS, WIDTH), vmem(POS, WIDTH), vmem(3, WIDTH, POS), vmem(4, POS, 2 * POS),
        vmem(4, HEADS, POS, D), vmem(HEADS, 8, POS, 2 * D), vmem32(8, 8, 128), vmem(8, POS, D),
        vmem32(*units, RC, D), vmem32(*units, 4, RC, D),
        vmem(*units, 3, RC, D), vmem(*units, HALF, D), vmem(*units, HALF, D),
        vmem(*units, RC, D), vmem(*units, RC, D), vmem(len(DIRECT), RC, D), vmem(*units, 2, HALF, D),
        vmem32(*units, 3, 1, RC), vmem32(*units, 1, RC), vmem32(*units, 1, RC), vmem32(*units, 1, RC),
        vmem32(len(DIRECT), 1, RC), vmem32(*units, 1, RC),
        vmem(4, *units, RC, D), vmem32(CH, RC, POS), vmem(CH, RC, POS), vmem(CH, RC, POS),
        pltpu.SemaphoreType.DMA((CH + 4,)),
        pltpu.SemaphoreType.DMA((MESSAGES,)),
        pltpu.SemaphoreType.DMA((MESSAGES,)),
    ]
    in_hbm = pl.BlockSpec(memory_space=pl.ANY)
    in_vmem = pl.BlockSpec(memory_space=pltpu.VMEM)
    return pl.pallas_call(
        kernel,
        out_shape=jax.ShapeDtypeStruct((POS, POS), bf16),
        in_specs=[in_hbm, in_vmem, in_vmem, in_hbm, in_vmem, in_hbm],
        out_specs=in_vmem,
        scratch_shapes=scratch,
        compiler_params=pltpu.CompilerParams(
            collective_id=0, has_side_effects=True, vmem_limit_bytes=60 * 2**20
        ),
        name="branch",
    )(
        tokens,
        survive.reshape(CH, RC),
        norm_gain.reshape(1, WIDTH),
        jnp.transpose(w_qkv, (1, 0, 2)),
        jnp.transpose(qk_gain, (1, 0, 2)),
        w_out,
    )


def solution(mesh):
    placed = (
        P("seq", None),
        P("seq"),
        P(),
        P(None, None, "head"),
        P(None, "head", None),
        P("head", None),
    )
    return jax.shard_map(
        per_device, mesh=mesh, in_specs=placed, out_specs=P("seq", "head"), check_vma=False
    )
```

```python
import math

import jax
import jax.numpy as jnp
from jax import lax
from jax.experimental import pallas as pl
from jax.experimental.pallas import tpu as pltpu
from jax.sharding import PartitionSpec as P

epsilon = 1e-06
MESH = pl.DeviceIdType.MESH
f32, bf16 = jnp.float32, jnp.bfloat16

POS = 384
WIDTH = 3072
HEADS = 3
D = 128
CH = 3
RC = POS // CH
HALF = RC // 2
LAST = HEADS - 1
PIECES = [(0, 0, RC), (1, 0, RC), (2, 0, RC)]


def column_of(row):
    return jnp.transpose(jnp.broadcast_to(row, (128, 128)))


def head_norm(x, gain):
    center = x - jnp.mean(x, axis=-1, keepdims=True)
    spread = jnp.mean(center * center, axis=-1, keepdims=True)
    return center * lax.rsqrt(spread + epsilon) * gain


def kernel(
    tok_hbm, sv_hbm, ng_hbm, w_hbm, qg_hbm, wo_hbm, out_ref,
    sv_ref, ng_ref, qg_ref,
    tok, normed, w, wo, q, kv, lrow, lv, own, dn,
    zs, zra, zrb, zfm, zfp, zff, zt, ds, dra, dfm, dfp, dt, dps, dpf,
    xa, total, given, zls, zlr,
    lsem, ssem, rsem,
):
    s = lax.axis_index("seq")
    hd = lax.axis_index("head")
    y, zh, co = s // 8, (s // 2) % 4, s % 2
    x, zl = hd // 2, hd % 2

    def seq_at(dy, dz, flip):
        c = (1 - co) if flip else co
        return {"seq": (((y + dy) % 4) * 4 + (zh + dz) % 4) * 2 + c}

    y_next, y_prev, sib = seq_at(1, 0, False), seq_at(3, 0, False), seq_at(0, 0, True)
    z_next, z_prev, z_far = (seq_at(0, dz, False) for dz in (1, 3, 2))
    x_next, x_prev, x_far = ({"head": ((x + dx) % 4) * 2 + zl} for dx in (1, 3, 2))
    z_pair = {"head": x * 2 + (1 - zl)}
    line = [
        (sib, 1), (y_next, 2), (seq_at(1, 0, True), 3), (y_prev, 4),
        (seq_at(3, 0, True), 5), (seq_at(2, 0, False), 6), (seq_at(2, 0, True), 7),
    ]

    token_loads = []
    for c in range(CH):
        rows = pl.ds(c * RC, RC)
        token_loads.append(pltpu.make_async_copy(tok_hbm.at[rows], tok.at[rows], lsem.at[c]))
    w_loads = [pltpu.make_async_copy(w_hbm.at[j], w.at[j], lsem.at[CH + j]) for j in range(3)]
    x_cols = lambda dx: pl.ds(pl.multiple_of(((x + dx) % 4) * 2 * POS, 128), 2 * POS)
    wo_load = pltpu.make_async_copy(wo_hbm.at[:, x_cols(0)], wo.at[0], lsem.at[CH + 3])
    small_loads = [
        pltpu.make_async_copy(src, dst, lsem.at[CH + 4 + i])
        for i, (src, dst) in enumerate(((ng_hbm, ng_ref), (sv_hbm, sv_ref), (qg_hbm, qg_ref)))
    ]
    for load in token_loads[0:1] + small_loads + token_loads[1:] + w_loads[0:1]:
        load.start()

    barrier = pltpu.get_barrier_semaphore()
    peers = [p for p, _ in line] + [z_next, z_prev, z_far, x_next, x_prev, x_far, z_pair]
    for peer in peers:
        pl.semaphore_signal(barrier, inc=1, device_id=peer, device_id_type=MESH)

    count = [0]
    sent = []

    def message(src, dst, peer):
        i = count[0]
        count[0] += 1
        copy = pltpu.make_async_remote_copy(
            src_ref=src, dst_ref=dst, send_sem=ssem.at[i], recv_sem=rsem.at[i],
            device_id=peer, device_id_type=MESH,
        )
        sent.append(copy)
        return copy


    def spread_live(slot):
        for t in range(CH):
            lv[slot, t * RC : (t + 1) * RC, :] = column_of(lrow[slot, t : t + 1, :]).astype(bf16)

    def norm_rows(i, carry):
        rows = pl.ds(pl.multiple_of(i * 32, 32), 32)
        v = tok[rows, :].astype(f32)
        center = v - jnp.mean(v, axis=-1, keepdims=True)
        spread = jnp.mean(center * center, axis=-1, keepdims=True)
        normed[rows, :] = (center * lax.rsqrt(spread + epsilon) * ng_ref[...]).astype(bf16)
        return carry

    score_scale = math.log2(math.e) / math.sqrt(D)
    lo, hi = pl.ds(0, POS // 2), pl.ds(POS // 2, POS // 2)
    q_next, q_prev, q_fwd_next, q_fwd_prev = [], [], [], []
    for c in range(CH):
        rows = pl.ds(c * RC, RC)
        first, second = pl.ds(c * RC, HALF), pl.ds(c * RC + HALF, HALF)
        q_next.append(message(q.at[0, :, rows], q.at[1, :, rows], z_next))
        q_prev.append(message(q.at[0, :, rows], q.at[2, :, rows], z_prev))
        q_fwd_next.append(message(q.at[1, :, first], q.at[3, :, first], z_next))
        q_fwd_prev.append(message(q.at[2, :, second], q.at[3, :, second], z_prev))

    def project_q(c):
        rows = slice(c * RC, (c + 1) * RC)
        projected = jnp.dot(normed[rows, :], w[0], preferred_element_type=f32)
        for h in range(HEADS):
            gain = qg_ref[h, 0:1, :] * score_scale
            q[0, h, rows, :] = head_norm(projected[:, h * D : (h + 1) * D], gain).astype(bf16)

    def send_q(c):
        q_next[c].start()
        q_prev[c].start()

    for load in small_loads:
        load.wait()
    lrow[0] = jnp.zeros((8, 128), f32)
    lrow[0, 0:CH, :] = (sv_ref[...] == 1).astype(f32)
    for c in range(CH):
        token_loads[c].wait()
        if c == 1:
            for load in w_loads[1:] + [wo_load]:
                load.start()
        lax.fori_loop(c * RC // 32, (c + 1) * RC // 32, norm_rows, 0)
        if c == 0:
            w_loads[0].wait()
            project_q(0)
            pl.semaphore_wait(barrier, len(peers))
            send_q(0)

    live_msg = [message(lrow.at[0], lrow.at[slot], peer) for peer, slot in line]
    core_rows = pl.ds(pl.multiple_of(co * (POS // 2), 16), POS // 2)
    wo_msg = [
        message(wo_hbm.at[core_rows, x_cols(dx)], wo.at[r, core_rows], peer)
        for dx, r, peer in ((1, 1, x_next), (3, 2, x_prev), (2, 3, x_far))
    ]
    wo_sib = [message(wo.at[r, core_rows], wo.at[r, core_rows], sib) for r in (1, 2, 3)]

    kv_next = [[message(kv.at[h, 0, half], kv.at[h, 2, half], y_next) for half in (lo, hi)] for h in range(HEADS)]
    kv_prev = [[message(kv.at[h, 0, half], kv.at[h, 4, half], y_prev) for half in (hi, lo)] for h in range(HEADS)]
    kv_fwd_next = [message(kv.at[h, 2, lo], kv.at[h, 6, lo], y_next) for h in range(HEADS)]
    kv_fwd_prev = [message(kv.at[h, 4, hi], kv.at[h, 6, hi], y_prev) for h in range(HEADS)]
    kv_sib = [[message(kv.at[h, 2 * r], kv.at[h, 2 * r + 1], sib) for r in range(4)] for h in range(HEADS)]

    def send_kv(h, part):
        kv_next[h][part].start()
        kv_prev[h][part].start()

    def forward_q(c):
        q_next[c].wait_recv()
        q_fwd_next[c].start()
        q_prev[c].wait_recv()
        q_fwd_prev[c].start()

    def forward_kv(h):
        kv_next[h][0].wait_recv()
        kv_fwd_next[h].start()
        kv_prev[h][0].wait_recv()
        kv_fwd_prev[h].start()

    def share_near(h):
        kv_next[h][1].wait_recv()
        kv_sib[h][1].start()
        kv_prev[h][1].wait_recv()
        kv_sib[h][2].start()

    def share_far(h):
        kv_fwd_next[h].wait_recv()
        kv_fwd_prev[h].wait_recv()
        kv_sib[h][3].start()

    def queries_in(c):
        q_fwd_next[c].wait_recv()
        q_fwd_prev[c].wait_recv()

    def all_in(h):
        for m in kv_sib[h]:
            m.wait_recv()

    def project_kv(h):
        cols = pl.ds(h * D, D)
        weights = jnp.concatenate([w[1, :, cols], w[2, :, cols]], axis=1)
        projected = jnp.dot(normed[...], weights, preferred_element_type=f32)
        kv[h, 0, :, 0:D] = head_norm(projected[:, :D], qg_ref[h, 1:2, :]).astype(bf16)
        kv[h, 0, :, D:] = (projected[:, D:] * lv[0].astype(f32)).astype(bf16)

    for m in live_msg + wo_msg:
        m.start()
    spread_live(0)
    w_loads[1].wait()
    w_loads[2].wait()
    project_kv(0)
    send_kv(0, 0)
    send_kv(0, 1)
    kv_sib[0][0].start()
    project_q(1)
    send_q(1)
    project_q(2)
    project_kv(1)
    send_kv(1, 0)
    kv_sib[1][0].start()
    forward_q(0)
    send_q(2)
    project_kv(2)
    kv_sib[2][0].start()
    for m, (_, slot) in zip(live_msg[:3], line[:3]):
        m.wait_recv()
        spread_live(slot)
    forward_kv(0)
    send_kv(1, 1)
    send_kv(2, 0)
    for m, (_, slot) in zip(live_msg[3:], line[3:]):
        m.wait_recv()
        spread_live(slot)

    def attend(queries, h):
        keys = kv[h, :, :, 0:D].reshape(8 * POS, D)
        scores = lax.dot_general(queries, keys, (((1,), (1,)), ((), ())), preferred_element_type=f32)
        weights = jnp.exp2(scores).astype(bf16)
        values = jnp.concatenate([kv[h, :, :, D:].reshape(8 * POS, D), lv[...].reshape(8 * POS, D)], axis=1)
        return jnp.dot(weights, values, preferred_element_type=f32)

    def keep(acc, h, c, slot):
        if slot == 0:
            own[h, c] = acc[:, 0:D]
        else:
            zs[h, c, slot - 1] = acc[:, 0:D].astype(bf16)
        dn[h, c, slot] = acc[:, D:]

    def unit(h, c, slots):
        acc = attend(jnp.concatenate([q[slot, h, c * RC : (c + 1) * RC, :] for slot in slots], axis=0), h)
        for i, slot in enumerate(slots):
            keep(acc[i * RC : (i + 1) * RC], h, c, slot)

    def far_unit(h):
        acc = attend(q[3, h], h)
        for c in range(CH):
            keep(acc[c * RC : (c + 1) * RC], h, c, 3)

    A, B = pl.ds(0, HALF), pl.ds(HALF, HALF)
    zmsg, dmsg = {}, {}
    for h in range(LAST):
        for c in range(CH):
            zmsg[h, c] = [
                message(zs.at[h, c, 2, A], zra.at[h, c], z_next),
                message(zs.at[h, c, 2, B], zrb.at[h, c], z_prev),
                message(zs.at[h, c, 1, B], zfm.at[h, c, B], z_next),
                message(zs.at[h, c, 0, A], zfp.at[h, c, A], z_prev),
                message(zt.at[h, c, 0], zfm.at[h, c, A], z_next),
                message(zt.at[h, c, 1], zfp.at[h, c, B], z_prev),
            ]
            dmsg[h, c] = [
                message(ds.at[h, c, 2], dra.at[h, c], z_next),
                message(ds.at[h, c, 0], dfp.at[h, c], z_prev),
                message(dt.at[h, c], dfm.at[h, c], z_next),
            ]

    def part(p):
        c, row, n = PIECES[p]
        return c, pl.ds(row, n)

    for p in range(len(PIECES)):
        c, rows = part(p)
        zmsg[p] = [
            message(zs.at[LAST, c, 2, rows], zff.at[c, rows], z_far),
            message(zs.at[LAST, c, 1, rows], zfm.at[LAST, c, rows], z_next),
            message(zs.at[LAST, c, 0, rows], zfp.at[LAST, c, rows], z_prev),
        ]
        dmsg[p] = [
            message(dps.at[p, 2], dpf.at[p, 2], z_far),
            message(dps.at[p, 1], dpf.at[p, 1], z_next),
            message(dps.at[p, 0], dpf.at[p, 0], z_prev),
        ]

    def den_rows(d1, d2, d3):
        lane = lax.broadcasted_iota(jnp.int32, d1.shape, 1)
        mixed = jnp.where(lane == 0, d1, jnp.where(lane == 1, d2, d3))
        mixed = jnp.concatenate([mixed] * (RC // d1.shape[0]), axis=0)
        return jnp.transpose(mixed)[0:8, :]

    def z_near(h, c):
        for m in zmsg[h, c][2:4]:
            m.start()

    def z_first(h, c, sends):
        for m in zmsg[h, c][sends]:
            m.start()
        rows = den_rows(dn[h, c, 1], dn[h, c, 2], dn[h, c, 3])
        for i in range(3):
            ds[h, c, i] = rows[i : i + 1, :]
        for d in dmsg[h, c][:2]:
            d.start()

    def last_step(p):
        c, rows = part(p)
        n = PIECES[p][2]
        first = c * RC + PIECES[p][1]
        acc = attend(jnp.concatenate([q[slot, LAST, first : first + n, :] for slot in range(4)], axis=0), LAST)
        own[LAST, c, rows] = acc[0:n, 0:D]
        dn[LAST, c, 0, rows] = acc[0:n, D:]
        for slot in range(1, 4):
            zs[LAST, c, slot - 1, rows] = acc[slot * n : (slot + 1) * n, 0:D].astype(bf16)
        for m in zmsg[p]:
            m.start()
        dens = den_rows(*(acc[slot * n : (slot + 1) * n, D:] for slot in range(1, 4)))
        for i in range(3):
            dps[p, i] = dens[i : i + 1, :]
        for d in dmsg[p]:
            d.start()

    def z_relay(h, c):
        m = zmsg[h, c]
        m[0].wait_recv()
        zt[h, c, 0] = (zra[h, c].astype(f32) + zs[h, c, 1, 0:HALF].astype(f32)).astype(bf16)
        m[4].start()
        m[1].wait_recv()
        zt[h, c, 1] = (zrb[h, c].astype(f32) + zs[h, c, 0, HALF:].astype(f32)).astype(bf16)
        m[5].start()
        d = dmsg[h, c]
        d[0].wait_recv()
        dt[h, c] = dra[h, c] + ds[h, c, 1]
        d[2].start()

    xmsg = {}
    for h in range(LAST):
        for c in range(CH):
            xmsg[h, c] = [
                message(xa.at[0, h, c], xa.at[r, h, c], peer)
                for r, peer in ((3, x_far), (1, x_next), (2, x_prev))
            ]
    zlmsg = []
    for p in range(len(PIECES)):
        c, rows = part(p)
        xmsg[p] = [
            message(xa.at[0, LAST, c, rows], xa.at[r, LAST, c, rows], peer)
            for r, peer in ((3, x_far), (1, x_next), (2, x_prev))
        ]
        zlmsg.append(message(zls.at[c, rows], zlr.at[c, rows], z_pair))

    def attended(h, c):
        for m in dmsg[h, c][1:] + zmsg[h, c][2:]:
            m.wait_recv()
        num = own[h, c] + zfm[h, c].astype(f32) + zfp[h, c].astype(f32)
        den = dn[h, c, 0] + column_of(dfm[h, c] + dfp[h, c])
        xa[0, h, c] = (num / den).astype(bf16)
        for m in xmsg[h, c]:
            m.start()

    def last_attended(p):
        c, rows = part(p)
        for m in dmsg[p] + zmsg[p]:
            m.wait_recv()
        num = own[LAST, c, rows]
        for other in (zfm[LAST, c, rows], zfp[LAST, c, rows], zff[c, rows]):
            num = num + other.astype(f32)
        others = column_of(dpf[p, 0] + dpf[p, 1] + dpf[p, 2])
        den = dn[LAST, c, 0, rows] + others[0 : PIECES[p][2], :]
        xa[0, LAST, c, rows] = (num / den).astype(bf16)
        for m in xmsg[p]:
            m.start()

    other_cols = pl.ds(pl.multiple_of((1 - zl) * POS, 128), POS)
    own_cols = pl.ds(pl.multiple_of(zl * POS, 128), POS)

    split = LAST * D

    def project_early():
        for h in range(LAST):
            for c in range(CH):
                for m in xmsg[h, c]:
                    m.wait_recv()
        heads = jnp.concatenate(
            [xa[r, h].reshape(POS, D) for r in range(4) for h in range(LAST)], axis=1
        )
        for cols, acc in ((other_cols, given), (own_cols, total)):
            weights = wo[:, 0:split, cols].reshape(4 * split, POS)
            acc[...] = jnp.dot(heads, weights, preferred_element_type=f32).reshape(CH, RC, POS)

    def project_out(p):
        c, rows = part(p)
        for m in xmsg[p]:
            m.wait_recv()
        heads = jnp.concatenate([xa[r, LAST, c, rows] for r in range(4)], axis=1)
        theirs = wo[:, split:, other_cols].reshape(4 * D, POS)
        zls[c, rows] = (given[c, rows] + jnp.dot(heads, theirs, preferred_element_type=f32)).astype(bf16)
        zlmsg[p].start()
        mine = wo[:, split:, own_cols].reshape(4 * D, POS)
        total[c, rows] = total[c, rows] + jnp.dot(heads, mine, preferred_element_type=f32)

    def finish(p):
        c, rows = part(p)
        zlmsg[p].wait_recv()
        first, n = c * RC + PIECES[p][1], PIECES[p][2]
        mask = jnp.concatenate([lv[0, first : first + n, :].astype(f32)] * (POS // D), axis=1)
        share = jnp.where(mask > 0.5, total[c, rows] + zlr[c, rows].astype(f32), 0.0)
        out_ref[first : first + n, :] = share.astype(bf16)

    def share_weights():
        for m, share in zip(wo_msg, wo_sib):
            m.wait_recv()
            share.start()

    def step(h, c):
        unit(h, c, range(4))
        z_first(h, c, slice(0, 4))

    share_near(0)
    forward_q(1)
    forward_kv(1)
    send_kv(2, 1)
    share_far(0)
    all_in(0)
    unit(0, 0, range(3))
    z_near(0, 0)
    forward_q(2)
    share_near(1)
    forward_kv(2)
    unit(0, 1, range(3))
    z_near(0, 1)
    share_far(1)
    unit(0, 2, range(3))
    z_near(0, 2)
    share_near(2)
    for c in range(CH):
        queries_in(c)
    far_unit(0)
    for c in range(CH):
        z_first(0, c, slice(0, 2))
    all_in(1)
    step(1, 0)
    share_far(2)
    step(1, 1)
    z_relay(0, 0)
    z_relay(0, 1)
    share_weights()
    step(1, 2)
    z_relay(0, 2)
    z_relay(1, 0)
    all_in(2)
    last_step(0)
    z_relay(1, 1)
    last_step(1)
    z_relay(1, 2)
    last_step(2)
    for h in range(LAST):
        for c in range(CH):
            attended(h, c)
    wo_load.wait()
    for m in wo_sib:
        m.wait_recv()
    for p in range(len(PIECES)):
        last_attended(p)
    project_early()
    for p in range(len(PIECES)):
        project_out(p)
    for p in range(len(PIECES)):
        finish(p)
    for copy in sent:
        copy.wait_send()
    assert count[0] == MESSAGES


MESSAGES = 7 + 6 + 12 + 30 + 54 + 3 * 6 + 18 + 3 * 4


def per_device(tokens, survive, norm_gain, w_qkv, qk_gain, w_out):
    vmem = lambda *shape: pltpu.VMEM(shape, bf16)
    vmem32 = lambda *shape: pltpu.VMEM(shape, f32)
    units = (HEADS, CH)
    scratch = [
        pltpu.VMEM((CH, RC), jnp.int32), vmem32(1, WIDTH), vmem32(HEADS, 2, D),
        vmem(POS, WIDTH), vmem(POS, WIDTH), vmem(3, WIDTH, POS), vmem(4, POS, 2 * POS),
        vmem(4, HEADS, POS, D), vmem(HEADS, 8, POS, 2 * D), vmem32(8, 8, 128), vmem(8, POS, D),
        vmem32(*units, RC, D), vmem32(*units, 4, RC, D),
        vmem(*units, 3, RC, D), vmem(*units, HALF, D), vmem(*units, HALF, D),
        vmem(*units, RC, D), vmem(*units, RC, D), vmem(CH, RC, D), vmem(*units, 2, HALF, D),
        vmem32(*units, 3, 1, RC), vmem32(*units, 1, RC), vmem32(*units, 1, RC), vmem32(*units, 1, RC),
        vmem32(*units, 1, RC), vmem32(len(PIECES), 3, 1, RC), vmem32(len(PIECES), 3, 1, RC),
        vmem(4, *units, RC, D), vmem32(CH, RC, POS), vmem32(CH, RC, POS), vmem(CH, RC, POS), vmem(CH, RC, POS),
        pltpu.SemaphoreType.DMA((CH + 7,)),
        pltpu.SemaphoreType.DMA((MESSAGES,)),
        pltpu.SemaphoreType.DMA((MESSAGES,)),
    ]
    in_hbm = pl.BlockSpec(memory_space=pl.ANY)
    return pl.pallas_call(
        kernel,
        out_shape=jax.ShapeDtypeStruct((POS, POS), bf16),
        in_specs=[in_hbm] * 6,
        out_specs=pl.BlockSpec(memory_space=pltpu.VMEM),
        scratch_shapes=scratch,
        compiler_params=pltpu.CompilerParams(
            collective_id=0, has_side_effects=True, vmem_limit_bytes=52 * 2**20
        ),
        name="branch",
    )(
        tokens,
        survive.reshape(CH, RC),
        norm_gain.reshape(1, WIDTH),
        jnp.transpose(w_qkv, (1, 0, 2)),
        jnp.transpose(qk_gain, (1, 0, 2)),
        w_out,
    )


def solution(mesh):
    placed = (
        P("seq", None),
        P("seq"),
        P(),
        P(None, None, "head"),
        P(None, "head", None),
        P("head", None),
    )
    return jax.shard_map(
        per_device, mesh=mesh, in_specs=placed, out_specs=P("seq", "head"), check_vma=False
    )
```

```python
import math

import jax
import jax.numpy as jnp
from jax import lax
from jax.experimental import pallas as pl
from jax.experimental.pallas import tpu as pltpu
from jax.sharding import PartitionSpec as P

epsilon = 1e-06
MESH = pl.DeviceIdType.MESH
f32, bf16 = jnp.float32, jnp.bfloat16

POS = 384
WIDTH = 3072
HEADS = 3
D = 128
CH = 3
RC = POS // CH
HALF = RC // 2
LAST = HEADS - 1
PIECES = [(0, 0, RC), (1, 0, RC), (2, 0, RC)]


def column_of(row):
    return jnp.transpose(jnp.broadcast_to(row, (128, 128)))


def head_norm(x, gain):
    center = x - jnp.mean(x, axis=-1, keepdims=True)
    spread = jnp.mean(center * center, axis=-1, keepdims=True)
    return center * lax.rsqrt(spread + epsilon) * gain


def kernel(
    tok_hbm, sv_hbm, ng_hbm, w_hbm, qg_hbm, wo_hbm, out_ref,
    sv_ref, ng_ref, qg_ref,
    tok, normed, w, wo, q, kv, lrow, lv, own, dn,
    zs, zra, zrb, zfm, zfp, zff, zt, ds, dra, dfm, dfp, dt, dps, dpf,
    xa, total, given, zls, zlr,
    lsem, ssem, rsem,
):
    s = lax.axis_index("seq")
    hd = lax.axis_index("head")
    y, zh, co = s // 8, (s // 2) % 4, s % 2
    x, zl = hd // 2, hd % 2

    def seq_at(dy, dz, flip):
        c = (1 - co) if flip else co
        return {"seq": (((y + dy) % 4) * 4 + (zh + dz) % 4) * 2 + c}

    y_next, y_prev, sib = seq_at(1, 0, False), seq_at(3, 0, False), seq_at(0, 0, True)
    z_next, z_prev, z_far = (seq_at(0, dz, False) for dz in (1, 3, 2))
    x_next, x_prev, x_far = ({"head": ((x + dx) % 4) * 2 + zl} for dx in (1, 3, 2))
    z_pair = {"head": x * 2 + (1 - zl)}
    line = [
        (sib, 1), (y_next, 2), (seq_at(1, 0, True), 3), (y_prev, 4),
        (seq_at(3, 0, True), 5), (seq_at(2, 0, False), 6), (seq_at(2, 0, True), 7),
    ]

    token_loads = []
    for c in range(CH):
        rows = pl.ds(c * RC, RC)
        token_loads.append(pltpu.make_async_copy(tok_hbm.at[rows], tok.at[rows], lsem.at[c]))
    w_loads = [pltpu.make_async_copy(w_hbm.at[j], w.at[j], lsem.at[CH + j]) for j in range(3)]
    x_cols = lambda dx: pl.ds(pl.multiple_of(((x + dx) % 4) * 2 * POS, 128), 2 * POS)
    wo_load = pltpu.make_async_copy(wo_hbm.at[:, x_cols(0)], wo.at[0], lsem.at[CH + 3])
    small_loads = [
        pltpu.make_async_copy(src, dst, lsem.at[CH + 4 + i])
        for i, (src, dst) in enumerate(((ng_hbm, ng_ref), (sv_hbm, sv_ref), (qg_hbm, qg_ref)))
    ]
    for load in token_loads[0:1] + small_loads + token_loads[1:] + w_loads[0:1]:
        load.start()

    barrier = pltpu.get_barrier_semaphore()
    peers = [p for p, _ in line] + [z_next, z_prev, z_far, x_next, x_prev, x_far, z_pair]
    for peer in peers:
        pl.semaphore_signal(barrier, inc=1, device_id=peer, device_id_type=MESH)

    count = [0]
    sent = []

    def message(src, dst, peer):
        i = count[0]
        count[0] += 1
        copy = pltpu.make_async_remote_copy(
            src_ref=src, dst_ref=dst, send_sem=ssem.at[i], recv_sem=rsem.at[i],
            device_id=peer, device_id_type=MESH,
        )
        sent.append(copy)
        return copy


    def spread_live(slot):
        for t in range(CH):
            lv[slot, t * RC : (t + 1) * RC, :] = column_of(lrow[slot, t : t + 1, :]).astype(bf16)

    def norm_rows(i, carry):
        rows = pl.ds(pl.multiple_of(i * 32, 32), 32)
        v = tok[rows, :].astype(f32)
        center = v - jnp.mean(v, axis=-1, keepdims=True)
        spread = jnp.mean(center * center, axis=-1, keepdims=True)
        normed[rows, :] = (center * lax.rsqrt(spread + epsilon) * ng_ref[...]).astype(bf16)
        return carry

    score_scale = math.log2(math.e) / math.sqrt(D)
    lo, hi = pl.ds(0, POS // 2), pl.ds(POS // 2, POS // 2)
    q_next, q_prev, q_fwd_next, q_fwd_prev = [], [], [], []
    for c in range(CH):
        rows = pl.ds(c * RC, RC)
        first, second = pl.ds(c * RC, HALF), pl.ds(c * RC + HALF, HALF)
        q_next.append(message(q.at[0, :, rows], q.at[1, :, rows], z_next))
        q_prev.append(message(q.at[0, :, rows], q.at[2, :, rows], z_prev))
        q_fwd_next.append(message(q.at[1, :, first], q.at[3, :, first], z_next))
        q_fwd_prev.append(message(q.at[2, :, second], q.at[3, :, second], z_prev))

    def project_q(c):
        rows = slice(c * RC, (c + 1) * RC)
        projected = jnp.dot(normed[rows, :], w[0], preferred_element_type=f32)
        for h in range(HEADS):
            gain = qg_ref[h, 0:1, :] * score_scale
            q[0, h, rows, :] = head_norm(projected[:, h * D : (h + 1) * D], gain).astype(bf16)

    def send_q(c):
        q_next[c].start()
        q_prev[c].start()

    for load in small_loads:
        load.wait()
    lrow[0] = jnp.zeros((8, 128), f32)
    lrow[0, 0:CH, :] = (sv_ref[...] == 1).astype(f32)
    for c in range(CH):
        token_loads[c].wait()
        if c == 1:
            for load in w_loads[1:] + [wo_load]:
                load.start()
        lax.fori_loop(c * RC // 32, (c + 1) * RC // 32, norm_rows, 0)
        if c == 0:
            w_loads[0].wait()
            project_q(0)
            pl.semaphore_wait(barrier, len(peers))
            send_q(0)

    live_msg = [message(lrow.at[0], lrow.at[slot], peer) for peer, slot in line]
    core_rows = pl.ds(pl.multiple_of(co * (POS // 2), 16), POS // 2)
    wo_msg = [
        message(wo_hbm.at[core_rows, x_cols(dx)], wo.at[r, core_rows], peer)
        for dx, r, peer in ((1, 1, x_next), (3, 2, x_prev), (2, 3, x_far))
    ]
    wo_sib = [message(wo.at[r, core_rows], wo.at[r, core_rows], sib) for r in (1, 2, 3)]

    kv_next = [[message(kv.at[h, 0, half], kv.at[h, 2, half], y_next) for half in (lo, hi)] for h in range(HEADS)]
    kv_prev = [[message(kv.at[h, 0, half], kv.at[h, 4, half], y_prev) for half in (hi, lo)] for h in range(HEADS)]
    kv_fwd_next = [message(kv.at[h, 2, lo], kv.at[h, 6, lo], y_next) for h in range(HEADS)]
    kv_fwd_prev = [message(kv.at[h, 4, hi], kv.at[h, 6, hi], y_prev) for h in range(HEADS)]
    kv_sib = [[message(kv.at[h, 2 * r], kv.at[h, 2 * r + 1], sib) for r in range(4)] for h in range(HEADS)]

    def send_kv(h, part):
        kv_next[h][part].start()
        kv_prev[h][part].start()

    def forward_q(c):
        q_next[c].wait_recv()
        q_fwd_next[c].start()
        q_prev[c].wait_recv()
        q_fwd_prev[c].start()

    def forward_kv(h):
        kv_next[h][0].wait_recv()
        kv_fwd_next[h].start()
        kv_prev[h][0].wait_recv()
        kv_fwd_prev[h].start()

    def share_near(h):
        kv_next[h][1].wait_recv()
        kv_sib[h][1].start()
        kv_prev[h][1].wait_recv()
        kv_sib[h][2].start()

    def share_far(h):
        kv_fwd_next[h].wait_recv()
        kv_fwd_prev[h].wait_recv()
        kv_sib[h][3].start()

    def queries_in(c):
        q_fwd_next[c].wait_recv()
        q_fwd_prev[c].wait_recv()

    def all_in(h):
        for m in kv_sib[h]:
            m.wait_recv()

    def project_kv(h):
        cols = pl.ds(h * D, D)
        weights = jnp.concatenate([w[1, :, cols], w[2, :, cols]], axis=1)
        projected = jnp.dot(normed[...], weights, preferred_element_type=f32)
        kv[h, 0, :, 0:D] = head_norm(projected[:, :D], qg_ref[h, 1:2, :]).astype(bf16)
        kv[h, 0, :, D:] = (projected[:, D:] * lv[0].astype(f32)).astype(bf16)

    for m in live_msg + wo_msg:
        m.start()
    spread_live(0)
    w_loads[1].wait()
    w_loads[2].wait()
    project_kv(0)
    send_kv(0, 0)
    send_kv(0, 1)
    kv_sib[0][0].start()
    project_q(1)
    send_q(1)
    project_q(2)
    project_kv(1)
    send_kv(1, 0)
    kv_sib[1][0].start()
    forward_q(0)
    send_q(2)
    project_kv(2)
    kv_sib[2][0].start()
    forward_kv(0)
    send_kv(1, 1)
    send_kv(2, 0)
    for m, (_, slot) in zip(live_msg, line):
        m.wait_recv()
        spread_live(slot)

    def attend(queries, h):
        keys = kv[h, :, :, 0:D].reshape(8 * POS, D)
        scores = lax.dot_general(queries, keys, (((1,), (1,)), ((), ())), preferred_element_type=f32)
        weights = jnp.exp2(scores).astype(bf16)
        values = jnp.concatenate([kv[h, :, :, D:].reshape(8 * POS, D), lv[...].reshape(8 * POS, D)], axis=1)
        return jnp.dot(weights, values, preferred_element_type=f32)

    def keep(acc, h, c, slot):
        if slot == 0:
            own[h, c] = acc[:, 0:D]
        else:
            zs[h, c, slot - 1] = acc[:, 0:D].astype(bf16)
        dn[h, c, slot] = acc[:, D:]

    def unit(h, c, slots):
        acc = attend(jnp.concatenate([q[slot, h, c * RC : (c + 1) * RC, :] for slot in slots], axis=0), h)
        for i, slot in enumerate(slots):
            keep(acc[i * RC : (i + 1) * RC], h, c, slot)

    def far_unit(h):
        acc = attend(q[3, h], h)
        for c in range(CH):
            keep(acc[c * RC : (c + 1) * RC], h, c, 3)

    A, B = pl.ds(0, HALF), pl.ds(HALF, HALF)
    zmsg, dmsg = {}, {}
    for h in range(LAST):
        for c in range(CH):
            zmsg[h, c] = [
                message(zs.at[h, c, 2, A], zra.at[h, c], z_next),
                message(zs.at[h, c, 2, B], zrb.at[h, c], z_prev),
                message(zs.at[h, c, 1, B], zfm.at[h, c, B], z_next),
                message(zs.at[h, c, 0, A], zfp.at[h, c, A], z_prev),
                message(zt.at[h, c, 0], zfm.at[h, c, A], z_next),
                message(zt.at[h, c, 1], zfp.at[h, c, B], z_prev),
            ]
            dmsg[h, c] = [
                message(ds.at[h, c, 2], dra.at[h, c], z_next),
                message(ds.at[h, c, 0], dfp.at[h, c], z_prev),
                message(dt.at[h, c], dfm.at[h, c], z_next),
            ]

    def part(p):
        c, row, n = PIECES[p]
        return c, pl.ds(row, n)

    for p in range(len(PIECES)):
        c, rows = part(p)
        zmsg[p] = [
            message(zs.at[LAST, c, 2, rows], zff.at[c, rows], z_far),
            message(zs.at[LAST, c, 1, rows], zfm.at[LAST, c, rows], z_next),
            message(zs.at[LAST, c, 0, rows], zfp.at[LAST, c, rows], z_prev),
        ]
        dmsg[p] = [
            message(dps.at[p, 2], dpf.at[p, 2], z_far),
            message(dps.at[p, 1], dpf.at[p, 1], z_next),
            message(dps.at[p, 0], dpf.at[p, 0], z_prev),
        ]

    def den_rows(d1, d2, d3):
        lane = lax.broadcasted_iota(jnp.int32, d1.shape, 1)
        mixed = jnp.where(lane == 0, d1, jnp.where(lane == 1, d2, d3))
        mixed = jnp.concatenate([mixed] * (RC // d1.shape[0]), axis=0)
        return jnp.transpose(mixed)[0:8, :]

    def z_near(h, c):
        for m in zmsg[h, c][2:4]:
            m.start()

    def z_first(h, c, sends):
        for m in zmsg[h, c][sends]:
            m.start()
        rows = den_rows(dn[h, c, 1], dn[h, c, 2], dn[h, c, 3])
        for i in range(3):
            ds[h, c, i] = rows[i : i + 1, :]
        for d in dmsg[h, c][:2]:
            d.start()

    def last_step(p):
        c, rows = part(p)
        n = PIECES[p][2]
        first = c * RC + PIECES[p][1]
        acc = attend(jnp.concatenate([q[slot, LAST, first : first + n, :] for slot in range(4)], axis=0), LAST)
        own[LAST, c, rows] = acc[0:n, 0:D]
        dn[LAST, c, 0, rows] = acc[0:n, D:]
        for slot in range(1, 4):
            zs[LAST, c, slot - 1, rows] = acc[slot * n : (slot + 1) * n, 0:D].astype(bf16)
        for m in zmsg[p]:
            m.start()
        dens = den_rows(*(acc[slot * n : (slot + 1) * n, D:] for slot in range(1, 4)))
        for i in range(3):
            dps[p, i] = dens[i : i + 1, :]
        for d in dmsg[p]:
            d.start()

    def z_relay(h, c):
        m = zmsg[h, c]
        m[0].wait_recv()
        zt[h, c, 0] = (zra[h, c].astype(f32) + zs[h, c, 1, 0:HALF].astype(f32)).astype(bf16)
        m[4].start()
        m[1].wait_recv()
        zt[h, c, 1] = (zrb[h, c].astype(f32) + zs[h, c, 0, HALF:].astype(f32)).astype(bf16)
        m[5].start()
        d = dmsg[h, c]
        d[0].wait_recv()
        dt[h, c] = dra[h, c] + ds[h, c, 1]
        d[2].start()

    xmsg = {}
    for h in range(LAST):
        for c in range(CH):
            xmsg[h, c] = [
                message(xa.at[0, h, c], xa.at[r, h, c], peer)
                for r, peer in ((3, x_far), (1, x_next), (2, x_prev))
            ]
    zlmsg = []
    for p in range(len(PIECES)):
        c, rows = part(p)
        xmsg[p] = [
            message(xa.at[0, LAST, c, rows], xa.at[r, LAST, c, rows], peer)
            for r, peer in ((3, x_far), (1, x_next), (2, x_prev))
        ]
        zlmsg.append(message(zls.at[c, rows], zlr.at[c, rows], z_pair))

    def attended(h, c):
        for m in dmsg[h, c][1:] + zmsg[h, c][2:]:
            m.wait_recv()
        num = own[h, c] + zfm[h, c].astype(f32) + zfp[h, c].astype(f32)
        den = dn[h, c, 0] + column_of(dfm[h, c] + dfp[h, c])
        xa[0, h, c] = (num / den).astype(bf16)
        for m in xmsg[h, c]:
            m.start()

    def last_attended(p):
        c, rows = part(p)
        for m in dmsg[p] + zmsg[p]:
            m.wait_recv()
        num = own[LAST, c, rows]
        for other in (zfm[LAST, c, rows], zfp[LAST, c, rows], zff[c, rows]):
            num = num + other.astype(f32)
        others = column_of(dpf[p, 0] + dpf[p, 1] + dpf[p, 2])
        den = dn[LAST, c, 0, rows] + others[0 : PIECES[p][2], :]
        xa[0, LAST, c, rows] = (num / den).astype(bf16)
        for m in xmsg[p]:
            m.start()

    other_cols = pl.ds(pl.multiple_of((1 - zl) * POS, 128), POS)
    own_cols = pl.ds(pl.multiple_of(zl * POS, 128), POS)

    split = LAST * D

    def project_early():
        for h in range(LAST):
            for c in range(CH):
                for m in xmsg[h, c]:
                    m.wait_recv()
        heads = jnp.concatenate(
            [xa[r, h].reshape(POS, D) for r in range(4) for h in range(LAST)], axis=1
        )
        for cols, acc in ((other_cols, given), (own_cols, total)):
            weights = wo[:, 0:split, cols].reshape(4 * split, POS)
            acc[...] = jnp.dot(heads, weights, preferred_element_type=f32).reshape(CH, RC, POS)

    def project_out(p):
        c, rows = part(p)
        for m in xmsg[p]:
            m.wait_recv()
        heads = jnp.concatenate([xa[r, LAST, c, rows] for r in range(4)], axis=1)
        theirs = wo[:, split:, other_cols].reshape(4 * D, POS)
        zls[c, rows] = (given[c, rows] + jnp.dot(heads, theirs, preferred_element_type=f32)).astype(bf16)
        zlmsg[p].start()
        mine = wo[:, split:, own_cols].reshape(4 * D, POS)
        total[c, rows] = total[c, rows] + jnp.dot(heads, mine, preferred_element_type=f32)

    def finish(p):
        c, rows = part(p)
        zlmsg[p].wait_recv()
        first, n = c * RC + PIECES[p][1], PIECES[p][2]
        mask = jnp.concatenate([lv[0, first : first + n, :].astype(f32)] * (POS // D), axis=1)
        share = jnp.where(mask > 0.5, total[c, rows] + zlr[c, rows].astype(f32), 0.0)
        out_ref[first : first + n, :] = share.astype(bf16)

    def share_weights():
        for m, share in zip(wo_msg, wo_sib):
            m.wait_recv()
            share.start()

    def step(h, c):
        unit(h, c, range(4))
        z_first(h, c, slice(0, 4))

    share_near(0)
    forward_q(1)
    forward_kv(1)
    send_kv(2, 1)
    share_far(0)
    all_in(0)
    unit(0, 0, range(3))
    z_near(0, 0)
    forward_q(2)
    share_near(1)
    forward_kv(2)
    unit(0, 1, range(3))
    z_near(0, 1)
    share_far(1)
    unit(0, 2, range(3))
    z_near(0, 2)
    share_near(2)
    for c in range(CH):
        queries_in(c)
    far_unit(0)
    for c in range(CH):
        z_first(0, c, slice(0, 2))
    all_in(1)
    step(1, 0)
    share_far(2)
    step(1, 1)
    z_relay(0, 0)
    z_relay(0, 1)
    share_weights()
    step(1, 2)
    z_relay(0, 2)
    z_relay(1, 0)
    all_in(2)
    last_step(0)
    z_relay(1, 1)
    last_step(1)
    z_relay(1, 2)
    last_step(2)
    for h in range(LAST):
        for c in range(CH):
            attended(h, c)
    wo_load.wait()
    for m in wo_sib:
        m.wait_recv()
    for p in range(len(PIECES)):
        last_attended(p)
    project_early()
    for p in range(len(PIECES)):
        project_out(p)
    for p in range(len(PIECES)):
        finish(p)
    for copy in sent:
        copy.wait_send()
    assert count[0] == MESSAGES


MESSAGES = 7 + 6 + 12 + 30 + 54 + 3 * 6 + 18 + 3 * 4


def per_device(tokens, survive, norm_gain, w_qkv, qk_gain, w_out):
    vmem = lambda *shape: pltpu.VMEM(shape, bf16)
    vmem32 = lambda *shape: pltpu.VMEM(shape, f32)
    units = (HEADS, CH)
    scratch = [
        pltpu.VMEM((CH, RC), jnp.int32), vmem32(1, WIDTH), vmem32(HEADS, 2, D),
        vmem(POS, WIDTH), vmem(POS, WIDTH), vmem(3, WIDTH, POS), vmem(4, POS, 2 * POS),
        vmem(4, HEADS, POS, D), vmem(HEADS, 8, POS, 2 * D), vmem32(8, 8, 128), vmem(8, POS, D),
        vmem32(*units, RC, D), vmem32(*units, 4, RC, D),
        vmem(*units, 3, RC, D), vmem(*units, HALF, D), vmem(*units, HALF, D),
        vmem(*units, RC, D), vmem(*units, RC, D), vmem(CH, RC, D), vmem(*units, 2, HALF, D),
        vmem32(*units, 3, 1, RC), vmem32(*units, 1, RC), vmem32(*units, 1, RC), vmem32(*units, 1, RC),
        vmem32(*units, 1, RC), vmem32(len(PIECES), 3, 1, RC), vmem32(len(PIECES), 3, 1, RC),
        vmem(4, *units, RC, D), vmem32(CH, RC, POS), vmem32(CH, RC, POS), vmem(CH, RC, POS), vmem(CH, RC, POS),
        pltpu.SemaphoreType.DMA((CH + 7,)),
        pltpu.SemaphoreType.DMA((MESSAGES,)),
        pltpu.SemaphoreType.DMA((MESSAGES,)),
    ]
    in_hbm = pl.BlockSpec(memory_space=pl.ANY)
    return pl.pallas_call(
        kernel,
        out_shape=jax.ShapeDtypeStruct((POS, POS), bf16),
        in_specs=[in_hbm] * 6,
        out_specs=pl.BlockSpec(memory_space=pltpu.VMEM),
        scratch_shapes=scratch,
        compiler_params=pltpu.CompilerParams(
            collective_id=0, has_side_effects=True, vmem_limit_bytes=52 * 2**20
        ),
        name="branch",
    )(
        tokens,
        survive.reshape(CH, RC),
        norm_gain.reshape(1, WIDTH),
        jnp.transpose(w_qkv, (1, 0, 2)),
        jnp.transpose(qk_gain, (1, 0, 2)),
        w_out,
    )


def solution(mesh):
    placed = (
        P("seq", None),
        P("seq"),
        P(),
        P(None, None, "head"),
        P(None, "head", None),
        P("head", None),
    )
    return jax.shard_map(
        per_device, mesh=mesh, in_specs=placed, out_specs=P("seq", "head"), check_vma=False
    )
```
